32 devices in a mesh: grp: 2 (over y), chan: 4 (over z), tm: 2 (over x), sub: 2 (over core).
Axes of the slice: x: 2, y: 2, z: 4, core: 2. Of those that a mesh axis runs over, the one named last changes fastest.
Arguments:
- raw: bfloat16 [1024, 16384], P(('grp', 'chan'), ('tm', 'sub')), parts along dimension 0, may hold values from -6 to 6
- fir_taps: bfloat16 [129], replicated, may hold values from -0.5 to 0.5
- spatial_taps: float32 [9], replicated, may hold values from -2 to 2
- band_edges: int32 [4], replicated, may hold values from 1 to 125, as said below
- source_owner: int32 [16], P('grp'), parts along dimension 0, may hold values from 0 to 3
- source_panel: int32 [8], replicated, may hold values from 0 to 3
- source_pick: int32 [8, 1024], P(None, ('grp', 'chan')), parts along dimension 1, may hold values from 0 to 31
Outputs:
- correlations: float32 [8, 1024, 128], P(None, ('grp', 'chan')), parts along dimension 1
The draws below stay inside these ranges and needn't reach their ends.
There are 2 independent parts, one for each index of `grp`. The reference program is written for one: setup_inputs(seed, part) draws one part's arguments, and reference() takes and returns one part's arrays. A program takes and returns all parts, laid end to end along the dimension named above; an argument that names none is the same for every part. Nothing has to cross between parts.
Inputs may be any that keep to these rules, and one draw needn't show every extreme that they name: `band_edges`: e0 < e1 <= e2 < e3, with e1 - e0 and e3 - e2 from 4 to 12.
All inputs are finite; a program needn't handle non-finite values.
Results may differ from the reference program's by a relative error of at most 0.0055.
Values may be sent and summed in bfloat16 or wider, within the bound.
A program may use at most 64 MiB of HBM per device.

```python
import math
import jax
import jax.numpy as jnp
from jax import lax

CB = 128
P_SIZE = 32
WIN = 256
TAPS = 129
SPAN = 9
LAGS = 128
REACH = 1000
STEPS = 8
CH = 512
SEGS = 4
SAMPLES = 16384
NW = 16
WT = 64
FREQS = 128
N_CHAN = 4


def draw_band_edges(key, part):
    streams = jax.random.split(key, 4)
    low_edge = jax.random.randint(streams[0], (), 1, 6)
    rise_len = jax.random.randint(streams[1], (), 4, 13)
    high_edge = jax.random.randint(streams[2], (), FREQS - 28, FREQS - 2)
    fall_len = jax.random.randint(streams[3], (), 4, 13)
    return jnp.stack([low_edge, low_edge + rise_len, high_edge - fall_len, high_edge]).astype(jnp.int32)


def with_ends(array, stream_key, smallest, largest):
    longest = array.shape.index(max(array.shape))
    spots = []
    for shift in (0, 1):
        where = [jax.random.randint(jax.random.fold_in(stream_key, axis), (), 0, length) for axis, length in enumerate(array.shape)]
        where[longest] = (where[longest] + shift) % array.shape[longest]
        spots.append(tuple(where))
    return array.at[spots[0]].set(smallest).at[spots[1]].set(largest)


def steps_of(own_key, shape, cuts, least, high):
    loudness = 1.0
    for position, parts in cuts:
        steps = jax.random.uniform(jax.random.fold_in(jax.random.fold_in(own_key, 6), position), (parts,), jnp.float32, least / len(cuts), high / len(cuts))
        loudness = loudness * jnp.repeat(jnp.exp(steps), shape[position] // parts).reshape((-1,) + (1,) * (len(shape) - 1 - position))
    return loudness


def centred(rng, dims, deviation, bound, cuts=(), dtype=jnp.bfloat16):
    level = steps_of(rng, dims, cuts, -0.22, 0.18) if cuts else 1.0
    values = jax.random.normal(rng, dims, jnp.float32) * deviation * level
    return jnp.minimum(jnp.maximum(values, -bound), bound).astype(dtype)


def setup_inputs(seed: int = 0, part: int = 0) -> dict:
    key_list = jax.random.split(jax.random.key(seed), 8)
    part_keys = jax.random.split(jax.random.fold_in(key_list[7], part), 8)
    raw = centred(part_keys[0], (CH, SAMPLES), 1.0, 6.0, ((0, 4), (1, 4)))
    fir_taps = centred(key_list[1], (TAPS,), TAPS ** -0.5, 0.5)
    spatial_taps = centred(key_list[2], (SPAN,), SPAN ** -0.5, 2.0, (), jnp.float32)
    band_edges = draw_band_edges(jax.random.fold_in(key_list[7], 71), part)
    source_owner = with_ends(jax.random.randint(part_keys[4], (STEPS,), 0, N_CHAN), jax.random.fold_in(part_keys[4], 1), 0, N_CHAN - 1).astype(jnp.int32)
    source_panel = with_ends(jax.random.randint(key_list[5], (STEPS,), 0, CB // P_SIZE), jax.random.fold_in(key_list[5], 1), 0, (CB // P_SIZE) - 1).astype(jnp.int32)
    source_pick = with_ends(jax.random.randint(part_keys[6], (STEPS, CH), 0, P_SIZE), jax.random.fold_in(part_keys[6], 1), 0, P_SIZE - 1).astype(jnp.int32)
    return {"raw": raw, "fir_taps": fir_taps, "spatial_taps": spatial_taps, "band_edges": band_edges, "source_owner": source_owner, "source_panel": source_panel, "source_pick": source_pick}


HIGHEST = lax.Precision.HIGHEST

def fir_matrix(fir_taps):
    tap_count = fir_taps.shape[0]
    row_index = jnp.arange(2 * (tap_count - 1))[:, None]
    col_index = jnp.arange(tap_count - 1)[None, :]
    offset = row_index - col_index
    is_valid = (offset >= 0) & (offset < tap_count)
    picked = jnp.take(fir_taps.astype(jnp.float32), jnp.clip(offset, 0, tap_count - 1))
    return jnp.where(is_valid, picked, jnp.float32(0.0))

def spectral_table(window_len):
    quarter = window_len // 4
    sample = jnp.arange(window_len)[:, None]
    column = jnp.arange(window_len)[None, :]
    bin_number = column // (2 * quarter) * quarter + column % quarter
    part_flag = column // quarter % 2
    phase = jnp.mod(bin_number * sample, window_len).astype(jnp.float32) * jnp.float32(2.0 * math.pi / window_len)
    entries = jnp.where(part_flag == 0, jnp.cos(phase), -jnp.sin(phase)) / jnp.float32(math.sqrt(window_len))
    return entries.astype(jnp.bfloat16)

def lag_matrix(first_half, halves, quarter, window_len, lag_count):
    column = jnp.arange(halves * 2 * quarter)[:, None]
    bin_number = (first_half + column // (2 * quarter)) * quarter + column % quarter
    part_flag = column // quarter % 2
    lag_shift = jnp.arange(lag_count)[None, :] - lag_count // 2
    phase = jnp.mod(bin_number * lag_shift, window_len).astype(jnp.float32) * jnp.float32(2.0 * math.pi / window_len)
    return jnp.where(part_flag == 0, jnp.cos(phase), -jnp.sin(phase)).astype(jnp.float32)

def band_taper(band_edges, bin_count):
    bin_values = jnp.arange(bin_count).astype(jnp.float32)
    edges = band_edges.astype(jnp.float32)
    rising = 0.5 - 0.5 * jnp.cos(jnp.float32(math.pi) * (bin_values - edges[0]) / (edges[1] - edges[0]))
    falling = 0.5 - 0.5 * jnp.cos(jnp.float32(math.pi) * (edges[3] - bin_values) / (edges[3] - edges[2]))
    inner = jnp.where(bin_values < edges[3], falling, jnp.float32(0.0))
    inner = jnp.where(bin_values <= edges[2], jnp.float32(1.0), inner)
    inner = jnp.where(bin_values < edges[1], rising, inner)
    return jnp.where(bin_values <= edges[0], jnp.float32(0.0), inner).astype(jnp.float32)

def whiten(spectra, band_edges):
    window_len = spectra.shape[-1]
    quarter = window_len // 4
    bin_count = window_len // 2
    leading = spectra.shape[:-1]
    split = spectra.reshape(leading + (2, 2, quarter))
    power = (split[..., 0, :] * split[..., 0, :] + split[..., 1, :] * split[..., 1, :]).reshape(leading + (bin_count,))
    mean_power = lax.optimization_barrier(jnp.mean(power, axis=-2))
    bin_values = jnp.arange(bin_count)
    smoother = (jnp.abs(bin_values[:, None] - bin_values[None, :]) <= 4).astype(jnp.float32)
    counts = lax.optimization_barrier(jnp.sum(smoother, axis=0))
    levels = jnp.dot(mean_power, smoother, precision=HIGHEST) / counts
    factor = band_taper(band_edges, bin_count) / jnp.sqrt(levels + 1e-06)
    factor = factor.reshape(factor.shape[:-1] + (2, 1, quarter))
    return (split * jnp.expand_dims(factor, -4)).astype(jnp.bfloat16)

def cross_terms(receiver_part, partner):
    recv_real = receiver_part[:, :, :, 0]
    recv_imag = receiver_part[:, :, :, 1]
    part_real = partner[:, :, :, 0]
    part_imag = partner[:, :, :, 1]
    real_sum = jnp.einsum('rwhf,rwhf->rhf', recv_real, part_real, precision=HIGHEST) + jnp.einsum('rwhf,rwhf->rhf', recv_imag, part_imag, precision=HIGHEST)
    imag_sum = jnp.einsum('rwhf,rwhf->rhf', recv_imag, part_real, precision=HIGHEST) - jnp.einsum('rwhf,rwhf->rhf', recv_real, part_imag, precision=HIGHEST)
    return jnp.stack([real_sum, imag_sum], axis=2).reshape(receiver_part.shape[0], -1)

def reference(raw, fir_taps, spatial_taps, band_edges, source_owner, source_panel, source_pick):
    channels, samples = raw.shape
    margin = (TAPS - 1) // 2
    padded = jnp.pad(raw.astype(jnp.float32), ((0, 0), (margin, margin)))
    blocks = padded.reshape(channels, samples // (2 * margin) + 1, 2 * margin)
    windows = jnp.concatenate([blocks[:, :-1], blocks[:, 1:]], axis=2)
    filtered = jnp.einsum('cbi,ij->cbj', windows, fir_matrix(fir_taps), precision=HIGHEST).reshape(channels, samples)
    side_len = SPAN // 2
    bordered = jnp.pad(filtered, ((side_len, side_len), (0, 0)))
    shaped = jnp.zeros_like(filtered)
    for tap_index in range(SPAN):
        shaped = shaped + spatial_taps[tap_index] * bordered[tap_index:tap_index + channels]
    shaped = shaped.astype(jnp.bfloat16)
    frames = shaped.astype(jnp.float32).reshape(channels, SEGS, NW, WIN)
    spectra = jnp.einsum('cgwn,nk->cgwk', frames, spectral_table(WIN).astype(jnp.float32), precision=HIGHEST)
    whitened = whiten(spectra, band_edges).astype(jnp.float32).reshape(channels, WT, 2, 2, WIN // 4)
    lag_table = lag_matrix(0, 2, WIN // 4, WIN, LAGS)
    norm_scale = 1.0 / math.sqrt(WT * FREQS)
    receivers = jnp.arange(channels).astype(jnp.int32)
    results = []
    for step_index in range(STEPS):
        start_row = (source_owner[step_index] * CB + source_panel[step_index] * P_SIZE).astype(jnp.int32)
        panel_rows = lax.dynamic_slice_in_dim(whitened, start_row, P_SIZE, 0)
        pick_row = source_pick[step_index].astype(jnp.int32)
        partner = jnp.take(panel_rows, pick_row, axis=0)
        cross_sum = cross_terms(whitened, partner)
        lagged = jnp.dot(cross_sum, lag_table, precision=HIGHEST) * norm_scale
        sources = start_row + pick_row
        nearby = jnp.abs(receivers - sources) <= REACH
        results.append(jnp.where(nearby[:, None], lagged, jnp.float32(0.0)))
    return jnp.stack(results)
```

```python
import functools
import math

import jax
import jax.numpy as jnp
import numpy as np
from jax import lax
from jax.experimental import pallas as pl
from jax.experimental.pallas import tpu as pltpu
from jax.sharding import PartitionSpec as P

P_SIZE = 32
WIN = 256
LAGS = 128
REACH = 1000
HIGHEST = lax.Precision.HIGHEST


def column_maps():
    column = np.arange(WIN)
    quarter = WIN // 4
    bins = column // (2 * quarter) * quarter + column % quarter
    parts = column // quarter % 2
    return bins, parts


def spectral_table():
    bins, parts = column_maps()
    angle = 2.0 * np.pi * ((bins[None, :] * np.arange(WIN)[:, None]) % WIN) / WIN
    table = np.where(parts == 0, np.cos(angle), -np.sin(angle)) / math.sqrt(WIN)
    return jnp.asarray(table.astype(np.float32)).astype(jnp.bfloat16)


def smooth_table():
    bins, _ = column_maps()
    near = np.abs(bins[:, None] - bins[None, :]) <= 4
    return jnp.asarray(near.astype(np.float32)), near.sum(0).astype(np.float32)[None, :] / 2.0


def lag_tables(scale):
    bins, parts = column_maps()
    lag = np.arange(LAGS) - LAGS // 2
    angle = 2.0 * np.pi * ((bins[:, None] * lag[None, :]) % WIN) / WIN
    real = np.cos(angle) * scale
    imag = np.where(parts[:, None] == 0, -np.sin(angle), np.sin(angle)) * scale
    return jnp.asarray(real.astype(np.float32)), jnp.asarray(imag.astype(np.float32))


def shift_perm(count, step):
    return [(i, i + step) for i in range(count) if 0 <= i + step < count]


def taper_row(edges_ref):
    column = lax.broadcasted_iota(jnp.int32, (1, WIN), 1)
    quarter = WIN // 4
    bins = (column // (2 * quarter) * quarter + column % quarter).astype(jnp.float32)
    e0, e1, e2, e3 = [jnp.full((1, WIN), edges_ref[k]).astype(jnp.float32) for k in range(4)]
    rising = 0.5 - 0.5 * jnp.cos(math.pi * (bins - e0) / (e1 - e0))
    falling = 0.5 - 0.5 * jnp.cos(math.pi * (e3 - bins) / (e3 - e2))
    inner = jnp.where(bins < e3, falling, 0.0)
    inner = jnp.where(bins <= e2, 1.0, inner)
    inner = jnp.where(bins < e1, rising, inner)
    return jnp.where(bins <= e0, 0.0, inner)


def white_kernel(frames, channels, side, taps_ref, sp_ref, edges_ref, ext_ref, table_ref, near_ref,
                 count_ref, out_ref, filt, spec):
    depth = taps_ref.shape[1]
    rolled = pltpu.roll(jnp.broadcast_to(taps_ref[...], (WIN, depth)), 0, 1, stride=1, stride_axis=0)
    fir_t = rolled.astype(jnp.bfloat16)
    power = jnp.zeros((channels, WIN), jnp.float32)
    for w in range(frames):
        block = ext_ref[:, w * WIN : w * WIN + depth]
        got = lax.dot_general(block, fir_t, (((1,), (1,)), ((), ())), preferred_element_type=jnp.float32)
        slot = w % 2
        filt[slot, 8 : 8 + channels] = got[:channels]
        filt[slot, 8 - side : 8] = got[channels : channels + side]
        filt[slot, 8 + channels : 8 + channels + side] = got[channels + side : channels + 2 * side]
        shaped = sp_ref[0] * filt[slot, 8 - side : 8 - side + channels]
        for m in range(1, 2 * side + 1):
            shaped += sp_ref[m] * filt[slot, 8 - side + m : 8 - side + m + channels]
        spectra = jnp.dot(shaped.astype(jnp.bfloat16), table_ref[...], preferred_element_type=jnp.float32)
        spec[w] = spectra
        power += spectra * spectra
    level = jnp.dot(power, near_ref[...], precision=HIGHEST, preferred_element_type=jnp.float32)
    level = level / (count_ref[...] * frames)
    factor = taper_row(edges_ref) / jnp.sqrt(level + 1e-06)
    for w in range(frames):
        out_ref[w] = (spec[w] * factor).astype(jnp.bfloat16)


def cross_kernel(frames, channels, start_ref, pick_ref, white_ref, panel_ref, real_ref, imag_ref,
                 base_ref, out_ref, plain, swapped):
    step = pl.program_id(0)
    half = WIN // 2

    @pl.when(step == 0)
    def _():
        for w in range(frames):
            value = white_ref[w].astype(jnp.float32)
            plain[w] = value
            for h in range(2):
                swapped[w, :, h * half : (h + 1) * half] = pltpu.roll(
                    value[:, h * half : (h + 1) * half], half // 2, 1
                )

    rows = channels // 2
    start = start_ref[step]
    for r in range(2):
        here = slice(r * rows, (r + 1) * rows)
        pick = pick_ref[0, here]
        chosen = (pick == lax.broadcasted_iota(jnp.int32, (rows, P_SIZE), 1)).astype(jnp.bfloat16)
        acc_p = jnp.zeros((rows, WIN), jnp.float32)
        acc_q = jnp.zeros((rows, WIN), jnp.float32)
        for w in range(frames):
            partner = jnp.dot(chosen, panel_ref[0, w], preferred_element_type=jnp.float32)
            acc_p += plain[w, here] * partner
            acc_q += swapped[w, here] * partner
        lagged = jnp.dot(acc_p, real_ref[...], precision=HIGHEST, preferred_element_type=jnp.float32)
        lagged += jnp.dot(acc_q, imag_ref[...], precision=HIGHEST, preferred_element_type=jnp.float32)
        receiver = base_ref[0] + r * rows + lax.broadcasted_iota(jnp.int32, (rows, 1), 0)
        far = jnp.abs(receiver - (start + pick)) > REACH
        out_ref[0, here] = jnp.where(far, 0.0, lagged)


SMEM = pl.BlockSpec(memory_space=pltpu.SMEM)
VMEM = pl.BlockSpec(memory_space=pltpu.VMEM)


def shards(raw, fir_taps, spatial_taps, band_edges, source_owner, source_panel, source_pick):
    channels, samples = raw.shape
    margin = (fir_taps.shape[0] - 1) // 2
    side = spatial_taps.shape[0] // 2
    frames = samples // WIN
    steps = source_owner.shape[0]
    times = ("tm", "sub")
    count = lax.axis_size(times)
    low = lax.ppermute(raw[:, samples - margin :], times, shift_perm(count, 1))
    high = lax.ppermute(raw[:, :margin], times, shift_perm(count, -1))
    ext = jnp.concatenate([low, raw, high], axis=1)
    n_chan = lax.axis_size("chan")
    below = lax.ppermute(ext[channels - side :], "chan", shift_perm(n_chan, 1))
    above = lax.ppermute(ext[:side], "chan", shift_perm(n_chan, -1))
    spare = jnp.zeros((16 - 2 * side, ext.shape[1]), ext.dtype)
    ext = jnp.concatenate([ext, below, above, spare], axis=0)
    depth = WIN + 2 * margin
    taps = jnp.pad(fir_taps.astype(jnp.float32), (0, depth - fir_taps.shape[0]))[None, :]
    near, counts = smooth_table()
    white = pl.pallas_call(
        functools.partial(white_kernel, frames, channels, side),
        out_shape=jax.ShapeDtypeStruct((frames, channels, WIN), jnp.bfloat16),
        in_specs=[VMEM, SMEM, SMEM, VMEM, VMEM, VMEM, VMEM],
        out_specs=VMEM,
        scratch_shapes=[
            pltpu.VMEM((2, channels + 16, WIN), jnp.float32),
            pltpu.VMEM((frames, channels, WIN), jnp.float32),
        ],
        compiler_params=pltpu.CompilerParams(vmem_limit_bytes=32 * 2**20),
        name="white",
    )(taps, spatial_taps, band_edges, ext, spectral_table(), near, jnp.asarray(counts))

    me = lax.axis_index("chan")
    own = jnp.stack([
        jnp.where(
            source_owner[s] == me,
            lax.dynamic_slice_in_dim(white, source_panel[s] * P_SIZE, P_SIZE, 1),
            jnp.zeros((), white.dtype),
        )
        for s in range(steps)
    ])
    panels = lax.psum(own, "chan")

    total = frames * count
    real, imag = lag_tables(1.0 / math.sqrt(total * (WIN // 2)))
    start = source_owner * channels + source_panel * P_SIZE
    base = (me * channels)[None]
    lagged = pl.pallas_call(
        functools.partial(cross_kernel, frames, channels),
        grid=(steps,),
        out_shape=jax.ShapeDtypeStruct((steps, channels, LAGS), jnp.float32),
        in_specs=[
            SMEM,
            pl.BlockSpec((1, channels, 1), lambda s: (s, 0, 0)),
            pl.BlockSpec((frames, channels, WIN), lambda s: (0, 0, 0)),
            pl.BlockSpec((1, frames, P_SIZE, WIN), lambda s: (s, 0, 0, 0)),
            pl.BlockSpec((WIN, LAGS), lambda s: (0, 0)),
            pl.BlockSpec((WIN, LAGS), lambda s: (0, 0)),
            SMEM,
        ],
        out_specs=pl.BlockSpec((1, channels, LAGS), lambda s: (s, 0, 0)),
        scratch_shapes=[pltpu.VMEM((frames, channels, WIN), jnp.float32)] * 2,
        compiler_params=pltpu.CompilerParams(vmem_limit_bytes=32 * 2**20),
        name="cross",
    )(start, source_pick[:, :, None], white, panels, real, imag, base)
    return lax.psum(lagged, times)


def solution(mesh):
    placed = (
        P(("grp", "chan"), ("tm", "sub")),
        P(),
        P(),
        P(),
        P("grp"),
        P(),
        P(None, ("grp", "chan")),
    )
    return jax.shard_map(
        shards,
        mesh=mesh,
        in_specs=placed,
        out_specs=P(None, ("grp", "chan"), None),
        check_vma=False,
    )
```

```python
import functools
import math

import jax
import jax.numpy as jnp
import numpy as np
from jax import lax
from jax.experimental import pallas as pl
from jax.experimental.pallas import tpu as pltpu
from jax.sharding import PartitionSpec as P

P_SIZE = 32
WIN = 256
LAGS = 128
REACH = 1000
HIGHEST = lax.Precision.HIGHEST


def column_maps():
    column = np.arange(WIN)
    quarter = WIN // 4
    bins = column // (2 * quarter) * quarter + column % quarter
    parts = column // quarter % 2
    return bins, parts


def spectral_table():
    bins, parts = column_maps()
    angle = 2.0 * np.pi * ((bins[None, :] * np.arange(WIN)[:, None]) % WIN) / WIN
    table = np.where(parts == 0, np.cos(angle), -np.sin(angle)) / math.sqrt(WIN)
    return jnp.asarray(table.astype(np.float32)).astype(jnp.bfloat16)


def smooth_table():
    bins, _ = column_maps()
    near = np.abs(bins[:, None] - bins[None, :]) <= 4
    return jnp.asarray(near.astype(np.float32)), near.sum(0).astype(np.float32)[None, :] / 2.0


def lag_tables(scale):
    bins, parts = column_maps()
    lag = np.arange(LAGS) - LAGS // 2
    angle = 2.0 * np.pi * ((bins[:, None] * lag[None, :]) % WIN) / WIN
    real = np.cos(angle) * scale
    imag = np.where(parts[:, None] == 0, -np.sin(angle), np.sin(angle)) * scale
    return jnp.asarray(real.astype(np.float32)), jnp.asarray(imag.astype(np.float32))


def shift_perm(count, step):
    return [(i, i + step) for i in range(count) if 0 <= i + step < count]


def taper_row(edges_ref):
    column = lax.broadcasted_iota(jnp.int32, (1, WIN), 1)
    quarter = WIN // 4
    bins = (column // (2 * quarter) * quarter + column % quarter).astype(jnp.float32)
    e0, e1, e2, e3 = [jnp.full((1, WIN), edges_ref[k]).astype(jnp.float32) for k in range(4)]
    rising = 0.5 - 0.5 * jnp.cos(math.pi * (bins - e0) / (e1 - e0))
    falling = 0.5 - 0.5 * jnp.cos(math.pi * (e3 - bins) / (e3 - e2))
    inner = jnp.where(bins < e3, falling, 0.0)
    inner = jnp.where(bins <= e2, 1.0, inner)
    inner = jnp.where(bins < e1, rising, inner)
    return jnp.where(bins <= e0, 0.0, inner)


def white_kernel(frames, channels, side, steps, taps_ref, sp_ref, edges_ref, panel_ref, ext_ref, table_ref,
                 near_ref, count_ref, out_ref, own_ref, filt, spec):
    depth = taps_ref.shape[1]
    rolled = pltpu.roll(jnp.broadcast_to(taps_ref[...], (WIN, depth)), 0, 1, stride=1, stride_axis=0)
    fir_t = rolled.astype(jnp.bfloat16)
    power = jnp.zeros((channels, WIN), jnp.float32)
    for w in range(frames):
        block = ext_ref[:, w * WIN : w * WIN + depth]
        got = lax.dot_general(block, fir_t, (((1,), (1,)), ((), ())), preferred_element_type=jnp.float32)
        slot = w % 2
        filt[slot, 8 : 8 + channels] = got[:channels]
        filt[slot, 8 - side : 8] = got[channels : channels + side]
        filt[slot, 8 + channels : 8 + channels + side] = got[channels + side : channels + 2 * side]
        shaped = sp_ref[0] * filt[slot, 8 - side : 8 - side + channels]
        for m in range(1, 2 * side + 1):
            shaped += sp_ref[m] * filt[slot, 8 - side + m : 8 - side + m + channels]
        spectra = jnp.dot(shaped.astype(jnp.bfloat16), table_ref[...], preferred_element_type=jnp.float32)
        spec[w] = spectra
        power += spectra * spectra
    level = jnp.dot(power, near_ref[...], precision=HIGHEST, preferred_element_type=jnp.float32)
    level = level / (count_ref[...] * frames)
    factor = taper_row(edges_ref) / jnp.sqrt(level + 1e-06)
    for w in range(frames):
        out_ref[w] = (spec[w] * factor).astype(jnp.bfloat16)
    for s in range(steps):
        first = pl.multiple_of(panel_ref[s] * P_SIZE, P_SIZE)
        for w in range(frames):
            own_ref[s, w] = out_ref[w, pl.ds(first, P_SIZE)]


SPLIT = 4
LAG = 2
MESH = pl.DeviceIdType.MESH


def cross_kernel(frames, channels, steps, n_chan, n_tm, n_sub, owner_ref, panel_ref, pick_ref, white_ref, own_ref,
                 real_ref, imag_ref, out_ref, plain, swapped, in_low, in_high, to_high, to_low, own_lag,
                 sub_in, tm_in, done, sem_high, sem_low, got_low, got_high, sub_send, sub_recv,
                 tm_send, tm_recv, fin_send, fin_recv):
    me = lax.axis_index("chan")
    my_tm = lax.axis_index("tm")
    my_sub = lax.axis_index("sub")
    half = WIN // 2
    part = channels // n_sub
    group = frames // SPLIT
    chunks = steps * SPLIT

    barrier = pltpu.get_barrier_semaphore()
    peers = [{"chan": lax.rem(me + d, n_chan)} for d in (1, n_chan - 1)]
    peers += [{"tm": lax.rem(my_tm + d, n_tm)} for d in range(1, n_tm)]
    peers += [{"sub": lax.rem(my_sub + d, n_sub)} for d in range(1, n_sub)]
    for peer in peers:
        pl.semaphore_signal(barrier, inc=1, device_id=peer, device_id_type=MESH)
    pl.semaphore_wait(barrier, len(peers))

    def up(c):
        return pltpu.make_async_remote_copy(
            src_ref=to_high.at[c], dst_ref=in_low.at[c], send_sem=sem_high.at[c], recv_sem=got_low.at[c],
            device_id={"chan": lax.rem(me + 1, n_chan)}, device_id_type=MESH)

    def down(c):
        return pltpu.make_async_remote_copy(
            src_ref=to_low.at[c], dst_ref=in_high.at[c], send_sem=sem_low.at[c], recv_sem=got_high.at[c],
            device_id={"chan": lax.rem(me + n_chan - 1, n_chan)}, device_id_type=MESH)

    def sub_copy(s, d):
        to = lax.rem(my_sub + d, n_sub)
        return pltpu.make_async_remote_copy(
            src_ref=own_lag.at[s, pl.ds(to * part, part)], dst_ref=sub_in.at[s, d - 1],
            send_sem=sub_send.at[s, d - 1], recv_sem=sub_recv.at[s, d - 1],
            device_id={"sub": to}, device_id_type=MESH)

    def tm_copy(s, d):
        return pltpu.make_async_remote_copy(
            src_ref=tm_in.at[s, my_tm], dst_ref=tm_in.at[s, my_tm],
            send_sem=tm_send.at[s, d - 1], recv_sem=tm_recv.at[s, d - 1],
            device_id={"tm": lax.rem(my_tm + d, n_tm)}, device_id_type=MESH)

    def fin_copy(s, d):
        here = pl.ds(my_sub * part, part)
        return pltpu.make_async_remote_copy(
            src_ref=done.at[s, here], dst_ref=done.at[s, here],
            send_sem=fin_send.at[s, d - 1], recv_sem=fin_recv.at[s, d - 1],
            device_id={"sub": lax.rem(my_sub + d, n_sub)}, device_id_type=MESH)

    @pl.when(me == 0)
    def _():
        in_low[...] = jnp.zeros_like(in_low)

    @pl.when(me == n_chan - 1)
    def _():
        in_high[...] = jnp.zeros_like(in_high)

    def stage(c, arrived, leaving):
        s = lax.div(c, SPLIT)
        k = lax.rem(c, SPLIT)
        mine = jnp.full((P_SIZE, WIN), owner_ref[s], jnp.int32) == me
        for w in range(group):
            leaving[c, w] = jnp.where(mine, own_ref[s, k * group + w], arrived[c, w])

    def relay(t):
        c = t - LAG * me

        @pl.when((c >= 0) & (c < chunks))
        def _():
            @pl.when(me > 0)
            def _():
                up(c).wait_recv()

            @pl.when(me < n_chan - 1)
            def _():
                stage(c, in_low, to_high)
                up(c).start()

        e = t - LAG * (n_chan - 1 - me)

        @pl.when((e >= 0) & (e < chunks))
        def _():
            @pl.when(me < n_chan - 1)
            def _():
                down(e).wait_recv()

            @pl.when(me > 0)
            def _():
                stage(e, in_high, to_low)
                down(e).start()

    def compute(s):
        rows = channels // 2
        owner = owner_ref[s]
        where = jnp.full((P_SIZE, WIN), owner, jnp.int32)
        start = owner * channels + panel_ref[s] * P_SIZE
        chosen = []
        for r in range(2):
            pick = pick_ref[s, r * rows : (r + 1) * rows]
            chosen.append((pick == lax.broadcasted_iota(jnp.int32, (rows, P_SIZE), 1)).astype(jnp.bfloat16))
        for r in range(2):
            here = slice(r * rows, (r + 1) * rows)
            acc_p = jnp.zeros((rows, WIN), jnp.float32)
            acc_q = jnp.zeros((rows, WIN), jnp.float32)
            for w in range(frames):
                c = s * SPLIT + w // group
                value = jnp.where(where < me, in_low[c, w % group], in_high[c, w % group])
                value = jnp.where(where == me, own_ref[s, w], value)
                partner = jnp.dot(chosen[r], value, preferred_element_type=jnp.float32)
                acc_p += plain[w, here] * partner
                acc_q += swapped[w, here] * partner
            lagged = jnp.dot(acc_p, real_ref[...], precision=HIGHEST, preferred_element_type=jnp.float32)
            lagged += jnp.dot(acc_q, imag_ref[...], precision=HIGHEST, preferred_element_type=jnp.float32)
            receiver = me * channels + r * rows + lax.broadcasted_iota(jnp.int32, (rows, 1), 0)
            far = jnp.abs(receiver - (start + pick_ref[s, here])) > REACH
            own_lag[s, here] = jnp.where(far, 0.0, lagged)
        for d in range(1, n_sub):
            sub_copy(s, d).start()

    def sub_sum(s):
        total = own_lag[s, pl.ds(my_sub * part, part)]
        for d in range(1, n_sub):
            sub_copy(s, d).wait_recv()
            total += sub_in[s, d - 1]
        tm_in[s, my_tm] = total
        for d in range(1, n_tm):
            tm_copy(s, d).start()

    def tm_sum(s):
        for d in range(1, n_tm):
            tm_copy(s, d).wait_recv()
        total = tm_in[s, 0]
        for k in range(1, n_tm):
            total += tm_in[s, k]
        done[s, pl.ds(my_sub * part, part)] = total
        for d in range(1, n_sub):
            fin_copy(s, d).start()

    def finish(s):
        for d in range(1, n_sub):
            fin_copy(s, d).wait_recv()
        out_ref[s] = done[s]

    delay = -(-(n_chan - 1) * LAG // SPLIT)

    def turn(u, carry):
        for k in range(SPLIT):
            relay(u * SPLIT + k)

        @pl.when(u == 0)
        def _():
            for w in range(frames):
                value = white_ref[w].astype(jnp.float32)
                plain[w] = value
                for h in range(2):
                    swapped[w, :, h * half : (h + 1) * half] = pltpu.roll(
                        value[:, h * half : (h + 1) * half], half // 2, 1)

        for late, work in enumerate((compute, sub_sum, tm_sum, finish)):
            s = u - delay - late
            pl.when((s >= 0) & (s < steps))(functools.partial(work, s))
        return carry

    lax.fori_loop(0, steps + delay + 3, turn, 0)

    def drain_chunk(c, carry):
        @pl.when(me < n_chan - 1)
        def _():
            up(c).wait_send()

        @pl.when(me > 0)
        def _():
            down(c).wait_send()
        return carry

    lax.fori_loop(0, chunks, drain_chunk, 0)

    def drain_step(s, carry):
        for d in range(1, n_sub):
            sub_copy(s, d).wait_send()
            fin_copy(s, d).wait_send()
        for d in range(1, n_tm):
            tm_copy(s, d).wait_send()
        return carry

    lax.fori_loop(0, steps, drain_step, 0)


SMEM = pl.BlockSpec(memory_space=pltpu.SMEM)
VMEM = pl.BlockSpec(memory_space=pltpu.VMEM)


def shards(raw, fir_taps, spatial_taps, band_edges, source_owner, source_panel, source_pick):
    channels, samples = raw.shape
    margin = (fir_taps.shape[0] - 1) // 2
    side = spatial_taps.shape[0] // 2
    frames = samples // WIN
    steps = source_owner.shape[0]
    times = ("tm", "sub")
    count = lax.axis_size(times)
    low = lax.ppermute(raw[:, samples - margin :], times, shift_perm(count, 1))
    high = lax.ppermute(raw[:, :margin], times, shift_perm(count, -1))
    ext = jnp.concatenate([low, raw, high], axis=1)
    n_chan = lax.axis_size("chan")
    below = lax.ppermute(ext[channels - side :], "chan", shift_perm(n_chan, 1))
    above = lax.ppermute(ext[:side], "chan", shift_perm(n_chan, -1))
    spare = jnp.zeros((16 - 2 * side, ext.shape[1]), ext.dtype)
    ext = jnp.concatenate([ext, below, above, spare], axis=0)
    depth = WIN + 2 * margin
    taps = jnp.pad(fir_taps.astype(jnp.float32), (0, depth - fir_taps.shape[0]))[None, :]
    near, counts = smooth_table()
    white, own = pl.pallas_call(
        functools.partial(white_kernel, frames, channels, side, steps),
        out_shape=[
            jax.ShapeDtypeStruct((frames, channels, WIN), jnp.bfloat16),
            jax.ShapeDtypeStruct((steps, frames, P_SIZE, WIN), jnp.bfloat16),
        ],
        in_specs=[VMEM, SMEM, SMEM, SMEM, VMEM, VMEM, VMEM, VMEM],
        out_specs=[VMEM, VMEM],
        scratch_shapes=[
            pltpu.VMEM((2, channels + 16, WIN), jnp.float32),
            pltpu.VMEM((frames, channels, WIN), jnp.float32),
        ],
        compiler_params=pltpu.CompilerParams(vmem_limit_bytes=32 * 2**20),
        name="white",
    )(taps, spatial_taps, band_edges, source_panel, ext, spectral_table(), near, jnp.asarray(counts))

    total = frames * count
    real, imag = lag_tables(1.0 / math.sqrt(total * (WIN // 2)))
    n_tm, n_sub = lax.axis_size("tm"), lax.axis_size("sub")
    chunks = steps * SPLIT
    flow = pltpu.VMEM((chunks, frames // SPLIT, P_SIZE, WIN), jnp.bfloat16)
    part = channels // n_sub
    dma = pltpu.SemaphoreType.DMA
    return pl.pallas_call(
        functools.partial(cross_kernel, frames, channels, steps, n_chan, n_tm, n_sub),
        out_shape=jax.ShapeDtypeStruct((steps, channels, LAGS), jnp.float32),
        in_specs=[SMEM, SMEM, VMEM, VMEM, VMEM, VMEM, VMEM],
        out_specs=VMEM,
        scratch_shapes=[
            pltpu.VMEM((frames, channels, WIN), jnp.float32),
            pltpu.VMEM((frames, channels, WIN), jnp.float32),
            flow, flow, flow, flow,
            pltpu.VMEM((steps, channels, LAGS), jnp.float32),
            pltpu.VMEM((steps, n_sub - 1, part, LAGS), jnp.float32),
            pltpu.VMEM((steps, n_tm, part, LAGS), jnp.float32),
            pltpu.VMEM((steps, channels, LAGS), jnp.float32),
            dma((chunks,)), dma((chunks,)), dma((chunks,)), dma((chunks,)),
            dma((steps, n_sub - 1)), dma((steps, n_sub - 1)),
            dma((steps, n_tm - 1)), dma((steps, n_tm - 1)),
            dma((steps, n_sub - 1)), dma((steps, n_sub - 1)),
        ],
        compiler_params=pltpu.CompilerParams(
            vmem_limit_bytes=40 * 2**20, collective_id=0, has_side_effects=True),
        name="cross",
    )(source_owner, source_panel, source_pick[:, :, None], white, own, real, imag)


def solution(mesh):
    placed = (
        P(("grp", "chan"), ("tm", "sub")),
        P(),
        P(),
        P(),
        P("grp"),
        P(),
        P(None, ("grp", "chan")),
    )
    return jax.shard_map(
        shards,
        mesh=mesh,
        in_specs=placed,
        out_specs=P(None, ("grp", "chan"), None),
        check_vma=False,
    )
```

```python
import functools
import math

import jax
import jax.numpy as jnp
import numpy as np
from jax import lax
from jax.experimental import pallas as pl
from jax.experimental.pallas import tpu as pltpu
from jax.sharding import PartitionSpec as P

P_SIZE = 32
WIN = 256
LAGS = 128
REACH = 1000
HIGHEST = lax.Precision.HIGHEST


def column_maps():
    column = np.arange(WIN)
    quarter = WIN // 4
    bins = column // (2 * quarter) * quarter + column % quarter
    parts = column // quarter % 2
    return bins, parts


def spectral_table():
    bins, parts = column_maps()
    angle = 2.0 * np.pi * ((bins[None, :] * np.arange(WIN)[:, None]) % WIN) / WIN
    table = np.where(parts == 0, np.cos(angle), -np.sin(angle)) / math.sqrt(WIN)
    return jnp.asarray(table.astype(np.float32)).astype(jnp.bfloat16)


def smooth_table():
    bins, _ = column_maps()
    near = np.abs(bins[:, None] - bins[None, :]) <= 4
    return jnp.asarray(near.astype(np.float32)), near.sum(0).astype(np.float32)[None, :] / 2.0


def lag_tables(scale):
    bins, parts = column_maps()
    lag = np.arange(LAGS) - LAGS // 2
    angle = 2.0 * np.pi * ((bins[:, None] * lag[None, :]) % WIN) / WIN
    real = np.cos(angle) * scale
    imag = np.where(parts[:, None] == 0, -np.sin(angle), np.sin(angle)) * scale
    return jnp.asarray(real.astype(np.float32)), jnp.asarray(imag.astype(np.float32))


def shift_perm(count, step):
    return [(i, i + step) for i in range(count) if 0 <= i + step < count]


def taper_row(edges_ref):
    column = lax.broadcasted_iota(jnp.int32, (1, WIN), 1)
    quarter = WIN // 4
    bins = (column // (2 * quarter) * quarter + column % quarter).astype(jnp.float32)
    e0, e1, e2, e3 = [jnp.full((1, WIN), edges_ref[k]).astype(jnp.float32) for k in range(4)]
    rising = 0.5 - 0.5 * jnp.cos(math.pi * (bins - e0) / (e1 - e0))
    falling = 0.5 - 0.5 * jnp.cos(math.pi * (e3 - bins) / (e3 - e2))
    inner = jnp.where(bins < e3, falling, 0.0)
    inner = jnp.where(bins <= e2, 1.0, inner)
    inner = jnp.where(bins < e1, rising, inner)
    return jnp.where(bins <= e0, 0.0, inner)


LANES = 128
MESH = pl.DeviceIdType.MESH


def white_kernel(frames, channels, side, steps, n_chan, n_tm, n_sub, taps_ref, sp_ref, edges_ref, panel_ref,
                 raw_ref, table_ref, near_ref, count_ref, out_ref, own_ref, filt, spec, ext, time_in,
                 chan_out, chan_in, corner_out, corner_in, send_sem, recv_sem):
    me = lax.axis_index("chan")
    n_time = n_tm * n_sub
    now = lax.axis_index("tm") * n_sub + lax.axis_index("sub")
    samples = frames * WIN
    depth = taps_ref.shape[1]

    def peer(dc, dt):
        at = lax.rem(now + dt + n_time, n_time)
        return {"chan": lax.rem(me + dc + n_chan, n_chan), "tm": lax.div(at, n_sub), "sub": lax.rem(at, n_sub)}

    moves = [(0, 1), (0, -1), (1, 0), (-1, 0), (1, 1), (1, -1), (-1, 1), (-1, -1)]
    barrier = pltpu.get_barrier_semaphore()
    for dc, dt in moves:
        pl.semaphore_signal(barrier, inc=1, device_id=peer(dc, dt), device_id_type=MESH)

    ends = (slice(channels - side, channels), slice(0, side))
    sides = (slice(samples - LANES, samples), slice(0, LANES))
    for k in range(2):
        chan_out[k] = raw_ref[ends[k]]
        for h in range(2):
            corner_out[2 * k + h] = raw_ref[ends[k], sides[h]]

    def exists(dc, dt):
        return (me + dc >= 0) & (me + dc < n_chan) & (now + dt >= 0) & (now + dt < n_time)

    def copy(k):
        dc, dt = moves[k]
        if k < 2:
            src, dst = raw_ref.at[:, sides[k]], time_in.at[k]
        elif k < 4:
            src, dst = chan_out.at[k - 2], chan_in.at[k - 2]
        else:
            src, dst = corner_out.at[k - 4], corner_in.at[k - 4]
        return pltpu.make_async_remote_copy(
            src_ref=src, dst_ref=dst, send_sem=send_sem.at[k], recv_sem=recv_sem.at[k],
            device_id=peer(dc, dt), device_id_type=MESH)

    pl.semaphore_wait(barrier, len(moves))
    for k in (2, 3, 0, 1, 4, 5, 6, 7):
        pl.when(exists(*moves[k]))(lambda k=k: copy(k).start())

    ext[:channels, LANES : LANES + samples] = raw_ref[...]
    rolled = pltpu.roll(jnp.broadcast_to(taps_ref[...], (WIN, depth)), 0, 1, stride=1, stride_axis=0)
    fir_t = rolled.astype(jnp.bfloat16)

    for k, (dc, dt) in enumerate(moves):
        there = exists(-dc, -dt)
        pl.when(there)(lambda k=k: copy(k).wait_recv())
        buf, slot = (time_in, k) if k < 2 else (chan_in, k - 2) if k < 4 else (corner_in, k - 4)

        @pl.when(jnp.logical_not(there))
        def _():
            buf[slot] = jnp.zeros(buf.shape[1:], buf.dtype)

    def rows(low, high):
        width = low.shape[1]
        spare = jnp.zeros((16 - 2 * side, width), jnp.float32)
        both = [low.astype(jnp.float32), high.astype(jnp.float32), spare]
        return jnp.concatenate(both, axis=0).astype(jnp.bfloat16)

    high_at = LANES + samples
    ext[:channels, :LANES] = time_in[0]
    ext[:channels, high_at:] = time_in[1]
    ext[channels:, LANES:high_at] = rows(chan_in[0], chan_in[1])
    ext[channels:, :LANES] = rows(corner_in[0], corner_in[2])
    ext[channels:, high_at:] = rows(corner_in[1], corner_in[3])
    power = jnp.zeros((channels, WIN), jnp.float32)
    for w in range(frames):
        block = ext[:, w * WIN : w * WIN + depth]
        got = lax.dot_general(block, fir_t, (((1,), (1,)), ((), ())), preferred_element_type=jnp.float32)
        slot = w % 2
        filt[slot, 8 : 8 + channels] = got[:channels]
        filt[slot, 8 - side : 8] = got[channels : channels + side]
        filt[slot, 8 + channels : 8 + channels + side] = got[channels + side : channels + 2 * side]
        shaped = sp_ref[0] * filt[slot, 8 - side : 8 - side + channels]
        for m in range(1, 2 * side + 1):
            shaped += sp_ref[m] * filt[slot, 8 - side + m : 8 - side + m + channels]
        spectra = jnp.dot(shaped.astype(jnp.bfloat16), table_ref[...], preferred_element_type=jnp.float32)
        spec[w] = spectra
        power += spectra * spectra
    level = jnp.dot(power, near_ref[...], precision=HIGHEST, preferred_element_type=jnp.float32)
    level = level / (count_ref[...] * frames)
    factor = taper_row(edges_ref) / jnp.sqrt(level + 1e-06)
    for w in range(frames):
        out_ref[w] = (spec[w] * factor).astype(jnp.bfloat16)
    for s in range(steps):
        panel = jnp.full((P_SIZE, WIN), panel_ref[s], jnp.int32)
        for w in range(frames):
            value = out_ref[w, :P_SIZE]
            for k in range(1, channels // P_SIZE):
                value = jnp.where(panel == k, out_ref[w, k * P_SIZE : (k + 1) * P_SIZE], value)
            own_ref[s, w] = value
    for k, move in enumerate(moves):
        pl.when(exists(*move))(lambda k=k: copy(k).wait_send())


SPLIT = 4
LAG = 3


def cross_kernel(frames, channels, steps, n_chan, n_tm, n_sub, owner_ref, panel_ref, pick_ref, white_ref, own_ref,
                 real_ref, imag_ref, out_ref, plain, swapped, in_low, in_high, to_high, to_low, own_lag,
                 sub_in, tm_in, done, sem_high, sem_low, got_low, got_high, sub_send, sub_recv,
                 tm_send, tm_recv, fin_send, fin_recv):
    me = lax.axis_index("chan")
    my_tm = lax.axis_index("tm")
    my_sub = lax.axis_index("sub")
    half = WIN // 2
    part = channels // n_sub
    group = frames // SPLIT
    chunks = steps * SPLIT

    barrier = pltpu.get_barrier_semaphore()
    peers = [{"chan": lax.rem(me + d, n_chan)} for d in (1, n_chan - 1)]
    peers += [{"tm": lax.rem(my_tm + d, n_tm)} for d in range(1, n_tm)]
    peers += [{"sub": lax.rem(my_sub + d, n_sub)} for d in range(1, n_sub)]
    for peer in peers:
        pl.semaphore_signal(barrier, inc=1, device_id=peer, device_id_type=MESH)
    pl.semaphore_wait(barrier, len(peers))

    def up(c):
        return pltpu.make_async_remote_copy(
            src_ref=to_high.at[c], dst_ref=in_low.at[c], send_sem=sem_high.at[c], recv_sem=got_low.at[c],
            device_id={"chan": lax.rem(me + 1, n_chan)}, device_id_type=MESH)

    def down(c):
        return pltpu.make_async_remote_copy(
            src_ref=to_low.at[c], dst_ref=in_high.at[c], send_sem=sem_low.at[c], recv_sem=got_high.at[c],
            device_id={"chan": lax.rem(me + n_chan - 1, n_chan)}, device_id_type=MESH)

    def sub_copy(s, d):
        to = lax.rem(my_sub + d, n_sub)
        return pltpu.make_async_remote_copy(
            src_ref=own_lag.at[s, pl.ds(to * part, part)], dst_ref=sub_in.at[s, d - 1],
            send_sem=sub_send.at[s, d - 1], recv_sem=sub_recv.at[s, d - 1],
            device_id={"sub": to}, device_id_type=MESH)

    def tm_copy(s, d):
        return pltpu.make_async_remote_copy(
            src_ref=tm_in.at[s, my_tm], dst_ref=tm_in.at[s, my_tm],
            send_sem=tm_send.at[s, d - 1], recv_sem=tm_recv.at[s, d - 1],
            device_id={"tm": lax.rem(my_tm + d, n_tm)}, device_id_type=MESH)

    def fin_copy(s, d):
        here = pl.ds(my_sub * part, part)
        return pltpu.make_async_remote_copy(
            src_ref=done.at[s, here], dst_ref=done.at[s, here],
            send_sem=fin_send.at[s, d - 1], recv_sem=fin_recv.at[s, d - 1],
            device_id={"sub": lax.rem(my_sub + d, n_sub)}, device_id_type=MESH)

    @pl.when(me == 0)
    def _():
        in_low[...] = jnp.zeros_like(in_low)

    @pl.when(me == n_chan - 1)
    def _():
        in_high[...] = jnp.zeros_like(in_high)

    def stage(c, arrived, leaving):
        s = lax.div(c, SPLIT)
        k = lax.rem(c, SPLIT)
        mine = jnp.full((P_SIZE, WIN), owner_ref[s], jnp.int32) == me
        for w in range(group):
            leaving[c, w] = jnp.where(mine, own_ref[s, k * group + w], arrived[c, w])

    def relay(t):
        c = t - LAG * me

        @pl.when((c >= 0) & (c < chunks))
        def _():
            @pl.when(me > 0)
            def _():
                up(c).wait_recv()

            @pl.when(me < n_chan - 1)
            def _():
                stage(c, in_low, to_high)
                up(c).start()

        e = t - LAG * (n_chan - 1 - me)

        @pl.when((e >= 0) & (e < chunks))
        def _():
            @pl.when(me < n_chan - 1)
            def _():
                down(e).wait_recv()

            @pl.when(me > 0)
            def _():
                stage(e, in_high, to_low)
                down(e).start()

    def compute(s):
        rows = channels // 2
        owner = owner_ref[s]
        where = jnp.full((P_SIZE, WIN), owner, jnp.int32)
        start = owner * channels + panel_ref[s] * P_SIZE
        chosen = []
        for r in range(2):
            pick = pick_ref[s, r * rows : (r + 1) * rows]
            chosen.append((pick == lax.broadcasted_iota(jnp.int32, (rows, P_SIZE), 1)).astype(jnp.bfloat16))
        for r in range(2):
            here = slice(r * rows, (r + 1) * rows)
            acc_p = jnp.zeros((rows, WIN), jnp.float32)
            acc_q = jnp.zeros((rows, WIN), jnp.float32)
            for w in range(frames):
                c = s * SPLIT + w // group
                value = jnp.where(where < me, in_low[c, w % group], in_high[c, w % group])
                value = jnp.where(where == me, own_ref[s, w], value)
                partner = jnp.dot(chosen[r], value, preferred_element_type=jnp.float32)
                acc_p += plain[w, here] * partner
                acc_q += swapped[w, here] * partner
            lagged = jnp.dot(acc_p, real_ref[...], precision=HIGHEST, preferred_element_type=jnp.float32)
            lagged += jnp.dot(acc_q, imag_ref[...], precision=HIGHEST, preferred_element_type=jnp.float32)
            receiver = me * channels + r * rows + lax.broadcasted_iota(jnp.int32, (rows, 1), 0)
            far = jnp.abs(receiver - (start + pick_ref[s, here])) > REACH
            own_lag[s, here] = jnp.where(far, 0.0, lagged)
        for d in range(1, n_sub):
            sub_copy(s, d).start()

    def sub_sum(s):
        total = own_lag[s, pl.ds(my_sub * part, part)]
        for d in range(1, n_sub):
            sub_copy(s, d).wait_recv()
            total += sub_in[s, d - 1]
        tm_in[s, my_tm] = total
        for d in range(1, n_tm):
            tm_copy(s, d).start()

    def tm_sum(s):
        for d in range(1, n_tm):
            tm_copy(s, d).wait_recv()
        total = tm_in[s, 0]
        for k in range(1, n_tm):
            total += tm_in[s, k]
        done[s, pl.ds(my_sub * part, part)] = total
        for d in range(1, n_sub):
            fin_copy(s, d).start()

    def finish(s):
        for d in range(1, n_sub):
            fin_copy(s, d).wait_recv()
        out_ref[s] = done[s]

    delay = -(-(n_chan - 1) * LAG // SPLIT)

    def turn(u, carry):
        for k in range(SPLIT):
            relay(u * SPLIT + k)

        @pl.when(u == 0)
        def _():
            for w in range(frames):
                value = white_ref[w].astype(jnp.float32)
                plain[w] = value
                for h in range(2):
                    swapped[w, :, h * half : (h + 1) * half] = pltpu.roll(
                        value[:, h * half : (h + 1) * half], half // 2, 1)

        for late, work in enumerate((compute, sub_sum, tm_sum, finish)):
            s = u - delay - late
            pl.when((s >= 0) & (s < steps))(functools.partial(work, s))
        return carry

    lax.fori_loop(0, steps + delay + 3, turn, 0)

    def drain_chunk(c, carry):
        @pl.when(me < n_chan - 1)
        def _():
            up(c).wait_send()

        @pl.when(me > 0)
        def _():
            down(c).wait_send()
        return carry

    lax.fori_loop(0, chunks, drain_chunk, 0)

    def drain_step(s, carry):
        for d in range(1, n_sub):
            sub_copy(s, d).wait_send()
            fin_copy(s, d).wait_send()
        for d in range(1, n_tm):
            tm_copy(s, d).wait_send()
        return carry

    lax.fori_loop(0, steps, drain_step, 0)


SMEM = pl.BlockSpec(memory_space=pltpu.SMEM)
VMEM = pl.BlockSpec(memory_space=pltpu.VMEM)


def shards(raw, fir_taps, spatial_taps, band_edges, source_owner, source_panel, source_pick):
    channels, samples = raw.shape
    margin = (fir_taps.shape[0] - 1) // 2
    side = spatial_taps.shape[0] // 2
    frames = samples // WIN
    steps = source_owner.shape[0]
    times = ("tm", "sub")
    count = lax.axis_size(times)
    n_chan = lax.axis_size("chan")
    n_tm, n_sub = lax.axis_size("tm"), lax.axis_size("sub")
    depth = WIN + 2 * LANES
    first = LANES - margin
    taps = jnp.pad(fir_taps.astype(jnp.float32), (first, depth - first - fir_taps.shape[0]))[None, :]
    near, counts = smooth_table()
    white, own = pl.pallas_call(
        functools.partial(white_kernel, frames, channels, side, steps, n_chan, n_tm, n_sub),
        out_shape=[
            jax.ShapeDtypeStruct((frames, channels, WIN), jnp.bfloat16),
            jax.ShapeDtypeStruct((steps, frames, P_SIZE, WIN), jnp.bfloat16),
        ],
        in_specs=[VMEM, SMEM, SMEM, SMEM, VMEM, VMEM, VMEM, VMEM],
        out_specs=[VMEM, VMEM],
        scratch_shapes=[
            pltpu.VMEM((2, channels + 16, WIN), jnp.float32),
            pltpu.VMEM((frames, channels, WIN), jnp.float32),
            pltpu.VMEM((channels + 16, samples + 2 * LANES), jnp.bfloat16),
            pltpu.VMEM((2, channels, LANES), jnp.bfloat16),
            pltpu.VMEM((2, side, samples), jnp.bfloat16),
            pltpu.VMEM((2, side, samples), jnp.bfloat16),
            pltpu.VMEM((4, side, LANES), jnp.bfloat16),
            pltpu.VMEM((4, side, LANES), jnp.bfloat16),
            pltpu.SemaphoreType.DMA((8,)),
            pltpu.SemaphoreType.DMA((8,)),
        ],
        compiler_params=pltpu.CompilerParams(
            vmem_limit_bytes=32 * 2**20, collective_id=1, has_side_effects=True),
        name="white",
    )(taps, spatial_taps, band_edges, source_panel, raw, spectral_table(), near, jnp.asarray(counts))

    total = frames * count
    real, imag = lag_tables(1.0 / math.sqrt(total * (WIN // 2)))
    chunks = steps * SPLIT
    flow = pltpu.VMEM((chunks, frames // SPLIT, P_SIZE, WIN), jnp.bfloat16)
    part = channels // n_sub
    dma = pltpu.SemaphoreType.DMA
    return pl.pallas_call(
        functools.partial(cross_kernel, frames, channels, steps, n_chan, n_tm, n_sub),
        out_shape=jax.ShapeDtypeStruct((steps, channels, LAGS), jnp.float32),
        in_specs=[SMEM, SMEM, VMEM, VMEM, VMEM, VMEM, VMEM],
        out_specs=VMEM,
        scratch_shapes=[
            pltpu.VMEM((frames, channels, WIN), jnp.float32),
            pltpu.VMEM((frames, channels, WIN), jnp.float32),
            flow, flow, flow, flow,
            pltpu.VMEM((steps, channels, LAGS), jnp.float32),
            pltpu.VMEM((steps, n_sub - 1, part, LAGS), jnp.float32),
            pltpu.VMEM((steps, n_tm, part, LAGS), jnp.float32),
            pltpu.VMEM((steps, channels, LAGS), jnp.float32),
            dma((chunks,)), dma((chunks,)), dma((chunks,)), dma((chunks,)),
            dma((steps, n_sub - 1)), dma((steps, n_sub - 1)),
            dma((steps, n_tm - 1)), dma((steps, n_tm - 1)),
            dma((steps, n_sub - 1)), dma((steps, n_sub - 1)),
        ],
        compiler_params=pltpu.CompilerParams(
            vmem_limit_bytes=40 * 2**20, collective_id=0, has_side_effects=True),
        name="cross",
    )(source_owner, source_panel, source_pick[:, :, None], white, own, real, imag)


def solution(mesh):
    placed = (
        P(("grp", "chan"), ("tm", "sub")),
        P(),
        P(),
        P(),
        P("grp"),
        P(),
        P(None, ("grp", "chan")),
    )
    return jax.shard_map(
        shards,
        mesh=mesh,
        in_specs=placed,
        out_specs=P(None, ("grp", "chan"), None),
        check_vma=False,
    )
```

```python
import functools
import math

import jax
import jax.numpy as jnp
import numpy as np
from jax import lax
from jax.experimental import pallas as pl
from jax.experimental.pallas import tpu as pltpu
from jax.sharding import PartitionSpec as P

P_SIZE = 32
WIN = 256
LAGS = 128
REACH = 1000
HIGHEST = lax.Precision.HIGHEST


def column_maps():
    column = np.arange(WIN)
    quarter = WIN // 4
    bins = column // (2 * quarter) * quarter + column % quarter
    parts = column // quarter % 2
    return bins, parts


def spectral_table():
    bins, parts = column_maps()
    angle = 2.0 * np.pi * ((bins[None, :] * np.arange(WIN)[:, None]) % WIN) / WIN
    table = np.where(parts == 0, np.cos(angle), -np.sin(angle)) / math.sqrt(WIN)
    return jnp.asarray(table.astype(np.float32)).astype(jnp.bfloat16)


def bins_of(shape, axis):
    column = lax.broadcasted_iota(jnp.int32, shape, axis)
    quarter = WIN // 4
    return lax.div(column, 2 * quarter) * quarter + lax.rem(column, quarter)


def lag_tables(scale):
    bins, parts = column_maps()
    lag = np.arange(LAGS) - LAGS // 2
    angle = 2.0 * np.pi * ((bins[:, None] * lag[None, :]) % WIN) / WIN
    real = np.cos(angle) * scale
    imag = np.where(parts[:, None] == 0, -np.sin(angle), np.sin(angle)) * scale
    return jnp.asarray(np.concatenate([real, imag]).astype(np.float32))


def taper_row(edges_ref):
    bins = bins_of((1, WIN), 1).astype(jnp.float32)
    e0, e1, e2, e3 = [jnp.full((1, WIN), edges_ref[k]).astype(jnp.float32) for k in range(4)]
    rising = 0.5 - 0.5 * jnp.cos(math.pi * (bins - e0) / (e1 - e0))
    falling = 0.5 - 0.5 * jnp.cos(math.pi * (e3 - bins) / (e3 - e2))
    inner = jnp.where(bins < e3, falling, 0.0)
    inner = jnp.where(bins <= e2, 1.0, inner)
    inner = jnp.where(bins < e1, rising, inner)
    return jnp.where(bins <= e0, 0.0, inner)


LANES = 128
SPLIT = 8
LAG = 4
MESH = pl.DeviceIdType.MESH


def kernel(frames, channels, side, steps, n_chan, n_tm, n_sub, sp_ref, edges_ref, owner_ref, panel_ref,
           taps_ref, pick_ref, raw_ref, table_hbm, lag_hbm, out_ref,
           table_ref, lag_ref, filt, spec, ext, time_in, chan_out, chan_in, corner_out, corner_in, send_sem,
           recv_sem, load_sem, white_ref, own_ref, chosen, pick_wide, plain, swapped, in_low, in_high, to_high,
           to_low, own_lag, sub_in, tm_in, done, sem_high, sem_low, got_low, got_high, sub_send, sub_recv,
           tm_send, tm_recv, fin_send, fin_recv):
    my_tm = lax.axis_index("tm")
    my_sub = lax.axis_index("sub")
    loads = [
        pltpu.make_async_copy(table_hbm, table_ref, load_sem.at[0]),
        pltpu.make_async_copy(lag_hbm, lag_ref, load_sem.at[1]),
    ]
    for load in loads:
        load.start()
    me = lax.axis_index("chan")
    n_time = n_tm * n_sub
    now = lax.axis_index("tm") * n_sub + lax.axis_index("sub")
    samples = frames * WIN
    depth = taps_ref.shape[1]

    def peer(dc, dt):
        at = lax.rem(now + dt + n_time, n_time)
        return {"chan": lax.rem(me + dc + n_chan, n_chan), "tm": lax.div(at, n_sub), "sub": lax.rem(at, n_sub)}

    moves = [(0, 1), (0, -1), (1, 0), (-1, 0), (1, 1), (1, -1), (-1, 1), (-1, -1)]
    barrier = pltpu.get_barrier_semaphore()
    peers = [peer(dc, dt) for dc, dt in moves]
    peers += [{"tm": lax.rem(my_tm + d, n_tm)} for d in range(1, n_tm)]
    peers += [{"sub": lax.rem(my_sub + d, n_sub)} for d in range(1, n_sub)]
    for to in peers:
        pl.semaphore_signal(barrier, inc=1, device_id=to, device_id_type=MESH)

    ends = (slice(channels - side, channels), slice(0, side))
    sides = (slice(samples - LANES, samples), slice(0, LANES))
    for k in range(2):
        chan_out[k] = raw_ref[ends[k]]
        for h in range(2):
            corner_out[2 * k + h] = raw_ref[ends[k], sides[h]]

    def exists(dc, dt):
        return (me + dc >= 0) & (me + dc < n_chan) & (now + dt >= 0) & (now + dt < n_time)

    def copy(k):
        dc, dt = moves[k]
        if k < 2:
            src, dst = raw_ref.at[:, sides[k]], time_in.at[k]
        elif k < 4:
            src, dst = chan_out.at[k - 2], chan_in.at[k - 2]
        else:
            src, dst = corner_out.at[k - 4], corner_in.at[k - 4]
        return pltpu.make_async_remote_copy(
            src_ref=src, dst_ref=dst, send_sem=send_sem.at[k], recv_sem=recv_sem.at[k],
            device_id=peer(dc, dt), device_id_type=MESH)

    pl.semaphore_wait(barrier, len(peers))
    for k in (2, 3, 0, 1, 4, 5, 6, 7):
        pl.when(exists(*moves[k]))(lambda k=k: copy(k).start())

    ext[:channels, LANES : LANES + samples] = raw_ref[...]
    rolled = pltpu.roll(jnp.broadcast_to(taps_ref[...], (WIN, depth)), 0, 1, stride=1, stride_axis=0)
    fir_t = rolled.astype(jnp.bfloat16)
    near = (jnp.abs(bins_of((WIN, WIN), 0) - bins_of((WIN, WIN), 1)) <= 4).astype(jnp.float32)
    row_bins = bins_of((1, WIN), 1)
    count = jnp.minimum(row_bins + 4, WIN // 2 - 1) - jnp.maximum(row_bins - 4, 0) + 1
    turned = jnp.transpose(pick_ref[...].astype(jnp.float32))
    for s in range(steps):
        wide = jnp.broadcast_to(turned[:, s : s + 1], (channels, LANES)).astype(jnp.int32)
        pick_wide[s] = wide
        chosen[s] = (
            wide[:, :P_SIZE] == lax.broadcasted_iota(jnp.int32, (channels, P_SIZE), 1)
        ).astype(jnp.bfloat16)

    @pl.when(me == 0)
    def _():
        in_low[...] = jnp.zeros_like(in_low)

    @pl.when(me == n_chan - 1)
    def _():
        in_high[...] = jnp.zeros_like(in_high)

    for k, (dc, dt) in enumerate(moves):
        there = exists(-dc, -dt)
        pl.when(there)(lambda k=k: copy(k).wait_recv())
        buf, slot = (time_in, k) if k < 2 else (chan_in, k - 2) if k < 4 else (corner_in, k - 4)

        @pl.when(jnp.logical_not(there))
        def _():
            buf[slot] = jnp.zeros(buf.shape[1:], buf.dtype)

    def rows(low, high):
        width = low.shape[1]
        spare = jnp.zeros((16 - 2 * side, width), jnp.float32)
        both = [low.astype(jnp.float32), high.astype(jnp.float32), spare]
        return jnp.concatenate(both, axis=0).astype(jnp.bfloat16)

    high_at = LANES + samples
    ext[:channels, :LANES] = time_in[0]
    ext[:channels, high_at:] = time_in[1]
    ext[channels:, LANES:high_at] = rows(chan_in[0], chan_in[1])
    ext[channels:, :LANES] = rows(corner_in[0], corner_in[2])
    ext[channels:, high_at:] = rows(corner_in[1], corner_in[3])
    loads[0].wait()
    power = jnp.zeros((channels, WIN), jnp.float32)
    for w in range(frames):
        block = ext[:, w * WIN : w * WIN + depth]
        got = lax.dot_general(block, fir_t, (((1,), (1,)), ((), ())), preferred_element_type=jnp.float32)
        slot = w % 2
        filt[slot, 8 : 8 + channels] = got[:channels]
        filt[slot, 8 - side : 8] = got[channels : channels + side]
        filt[slot, 8 + channels : 8 + channels + side] = got[channels + side : channels + 2 * side]
        shaped = sp_ref[0] * filt[slot, 8 - side : 8 - side + channels]
        for m in range(1, 2 * side + 1):
            shaped += sp_ref[m] * filt[slot, 8 - side + m : 8 - side + m + channels]
        spectra = jnp.dot(shaped.astype(jnp.bfloat16), table_ref[...], preferred_element_type=jnp.float32)
        spec[w] = spectra
        power += spectra * spectra
    level = jnp.dot(power, near, precision=HIGHEST, preferred_element_type=jnp.float32)
    level = level / (count.astype(jnp.float32) * frames)
    factor = taper_row(edges_ref) / jnp.sqrt(level + 1e-06)
    for w in range(frames):
        white_ref[w] = (spec[w] * factor).astype(jnp.bfloat16)
    loads[1].wait()
    half = WIN // 2
    part = channels // n_sub
    group = frames // SPLIT
    chunks = steps * SPLIT

    def up(c):
        return pltpu.make_async_remote_copy(
            src_ref=to_high.at[c], dst_ref=in_low.at[c], send_sem=sem_high.at[c], recv_sem=got_low.at[c],
            device_id={"chan": lax.rem(me + 1, n_chan)}, device_id_type=MESH)

    def down(c):
        return pltpu.make_async_remote_copy(
            src_ref=to_low.at[c], dst_ref=in_high.at[c], send_sem=sem_low.at[c], recv_sem=got_high.at[c],
            device_id={"chan": lax.rem(me + n_chan - 1, n_chan)}, device_id_type=MESH)

    def sub_copy(s, d):
        to = lax.rem(my_sub + d, n_sub)
        return pltpu.make_async_remote_copy(
            src_ref=own_lag.at[s, pl.ds(to * part, part)], dst_ref=sub_in.at[s, d - 1],
            send_sem=sub_send.at[s, d - 1], recv_sem=sub_recv.at[s, d - 1],
            device_id={"sub": to}, device_id_type=MESH)

    def tm_copy(s, d):
        return pltpu.make_async_remote_copy(
            src_ref=tm_in.at[s, my_tm], dst_ref=tm_in.at[s, my_tm],
            send_sem=tm_send.at[s, d - 1], recv_sem=tm_recv.at[s, d - 1],
            device_id={"tm": lax.rem(my_tm + d, n_tm)}, device_id_type=MESH)

    def fin_copy(s, d):
        here = pl.ds(my_sub * part, part)
        return pltpu.make_async_remote_copy(
            src_ref=done.at[s, here], dst_ref=done.at[s, here],
            send_sem=fin_send.at[s, d - 1], recv_sem=fin_recv.at[s, d - 1],
            device_id={"sub": lax.rem(my_sub + d, n_sub)}, device_id_type=MESH)

    def own_panel(s):
        panel = jnp.full((P_SIZE, WIN), panel_ref[s], jnp.int32)
        for w in range(frames):
            value = white_ref[w, :P_SIZE]
            for k in range(1, channels // P_SIZE):
                value = jnp.where(panel == k, white_ref[w, k * P_SIZE : (k + 1) * P_SIZE], value)
            own_ref[s, w] = value

    def stage(c, arrived, leaving):
        s = lax.div(c, SPLIT)
        k = lax.rem(c, SPLIT)
        mine = jnp.full((P_SIZE, WIN), owner_ref[s], jnp.int32) == me
        for w in range(group):
            leaving[c, w] = jnp.where(mine, own_ref[s, k * group + w], arrived[c, w])

    def relay(t):
        c = t - LAG * me

        @pl.when((c >= 0) & (c < chunks))
        def _():
            @pl.when(me > 0)
            def _():
                up(c).wait_recv()

            @pl.when(me < n_chan - 1)
            def _():
                stage(c, in_low, to_high)
                up(c).start()

        e = t - LAG * (n_chan - 1 - me)

        @pl.when((e >= 0) & (e < chunks))
        def _():
            @pl.when(me < n_chan - 1)
            def _():
                down(e).wait_recv()

            @pl.when(me > 0)
            def _():
                stage(e, in_high, to_low)
                down(e).start()

    def compute(s):
        rows = channels // 2
        owner = owner_ref[s]
        where = jnp.full((P_SIZE, WIN), owner, jnp.int32)
        start = owner * channels + panel_ref[s] * P_SIZE
        for r in range(2):
            here = slice(r * rows, (r + 1) * rows)
            acc_p = jnp.zeros((rows, WIN), jnp.float32)
            acc_q = jnp.zeros((rows, WIN), jnp.float32)
            for w in range(frames):
                c = s * SPLIT + w // group
                value = jnp.where(where < me, in_low[c, w % group], in_high[c, w % group])
                value = jnp.where(where == me, own_ref[s, w], value)
                partner = jnp.dot(chosen[s, here], value, preferred_element_type=jnp.float32)
                acc_p += plain[w, here] * partner
                acc_q += swapped[w, here] * partner
            lagged = jnp.dot(acc_p, lag_ref[:WIN], precision=HIGHEST, preferred_element_type=jnp.float32)
            lagged += jnp.dot(acc_q, lag_ref[WIN:], precision=HIGHEST, preferred_element_type=jnp.float32)
            receiver = me * channels + r * rows + lax.broadcasted_iota(jnp.int32, (rows, LAGS), 0)
            far = jnp.abs(receiver - (start + pick_wide[s, here])) > REACH
            own_lag[s, here] = jnp.where(far, 0.0, lagged)
        for d in range(1, n_sub):
            sub_copy(s, d).start()

    def sub_sum(s):
        total = own_lag[s, pl.ds(my_sub * part, part)]
        for d in range(1, n_sub):
            sub_copy(s, d).wait_recv()
            total += sub_in[s, d - 1]
        tm_in[s, my_tm] = total
        for d in range(1, n_tm):
            tm_copy(s, d).start()

    def tm_sum(s):
        for d in range(1, n_tm):
            tm_copy(s, d).wait_recv()
        total = tm_in[s, 0]
        for k in range(1, n_tm):
            total += tm_in[s, k]
        done[s, pl.ds(my_sub * part, part)] = total
        for d in range(1, n_sub):
            fin_copy(s, d).start()

    def finish(s):
        for d in range(1, n_sub):
            fin_copy(s, d).wait_recv()
        out_ref[s] = done[s]

    delay = -(-(n_chan - 1) * LAG // SPLIT)

    def turn(u, carry):
        pl.when(u < steps)(functools.partial(own_panel, u))
        for k in range(SPLIT):
            relay(u * SPLIT + k)

        @pl.when(u == 0)
        def _():
            for w in range(frames):
                value = white_ref[w].astype(jnp.float32)
                plain[w] = value
                for h in range(2):
                    swapped[w, :, h * half : (h + 1) * half] = pltpu.roll(
                        value[:, h * half : (h + 1) * half], half // 2, 1)

        for late, work in enumerate((compute, sub_sum, tm_sum, finish)):
            s = u - delay - late
            pl.when((s >= 0) & (s < steps))(functools.partial(work, s))
        return carry

    lax.fori_loop(0, steps + delay + 3, turn, 0)

    def drain_chunk(c, carry):
        @pl.when(me < n_chan - 1)
        def _():
            up(c).wait_send()

        @pl.when(me > 0)
        def _():
            down(c).wait_send()
        return carry

    lax.fori_loop(0, chunks, drain_chunk, 0)
    for k, move in enumerate(moves):
        pl.when(exists(*move))(lambda k=k: copy(k).wait_send())

    def drain_step(s, carry):
        for d in range(1, n_sub):
            sub_copy(s, d).wait_send()
            fin_copy(s, d).wait_send()
        for d in range(1, n_tm):
            tm_copy(s, d).wait_send()
        return carry

    lax.fori_loop(0, steps, drain_step, 0)


SMEM = pl.BlockSpec(memory_space=pltpu.SMEM)
VMEM = pl.BlockSpec(memory_space=pltpu.VMEM)


def shards(raw, fir_taps, spatial_taps, band_edges, source_owner, source_panel, source_pick):
    channels, samples = raw.shape
    margin = (fir_taps.shape[0] - 1) // 2
    side = spatial_taps.shape[0] // 2
    frames = samples // WIN
    steps = source_owner.shape[0]
    times = ("tm", "sub")
    count = lax.axis_size(times)
    n_chan = lax.axis_size("chan")
    n_tm, n_sub = lax.axis_size("tm"), lax.axis_size("sub")
    depth = WIN + 2 * LANES
    first = LANES - margin
    taps = jnp.pad(fir_taps.astype(jnp.float32), (first, depth - first - fir_taps.shape[0]))[None, :]
    total = frames * n_tm * n_sub
    lag_table = lag_tables(1.0 / math.sqrt(total * (WIN // 2)))
    chunks = steps * SPLIT
    flow = pltpu.VMEM((chunks, frames // SPLIT, P_SIZE, WIN), jnp.bfloat16)
    part = channels // n_sub
    dma = pltpu.SemaphoreType.DMA
    any_space = pl.BlockSpec(memory_space=pl.ANY)
    bf16, f32 = jnp.bfloat16, jnp.float32
    return pl.pallas_call(
        functools.partial(kernel, frames, channels, side, steps, n_chan, n_tm, n_sub),
        out_shape=jax.ShapeDtypeStruct((steps, channels, LAGS), f32),
        in_specs=[SMEM, SMEM, SMEM, SMEM, VMEM, VMEM, VMEM, any_space, any_space],
        out_specs=VMEM,
        scratch_shapes=[
            pltpu.VMEM((WIN, WIN), bf16),
            pltpu.VMEM((2 * WIN, LAGS), f32),
            pltpu.VMEM((2, channels + 16, WIN), f32),
            pltpu.VMEM((frames, channels, WIN), f32),
            pltpu.VMEM((channels + 16, samples + 2 * LANES), bf16),
            pltpu.VMEM((2, channels, LANES), bf16),
            pltpu.VMEM((2, side, samples), bf16),
            pltpu.VMEM((2, side, samples), bf16),
            pltpu.VMEM((4, side, LANES), bf16),
            pltpu.VMEM((4, side, LANES), bf16),
            dma((8,)), dma((8,)), dma((2,)),
            pltpu.VMEM((frames, channels, WIN), bf16),
            pltpu.VMEM((steps, frames, P_SIZE, WIN), bf16),
            pltpu.VMEM((steps, channels, P_SIZE), bf16),
            pltpu.VMEM((steps, channels, LANES), jnp.int32),
            pltpu.VMEM((frames, channels, WIN), f32),
            pltpu.VMEM((frames, channels, WIN), f32),
            flow, flow, flow, flow,
            pltpu.VMEM((steps, channels, LAGS), f32),
            pltpu.VMEM((steps, n_sub - 1, part, LAGS), f32),
            pltpu.VMEM((steps, n_tm, part, LAGS), f32),
            pltpu.VMEM((steps, channels, LAGS), f32),
            dma((chunks,)), dma((chunks,)), dma((chunks,)), dma((chunks,)),
            dma((steps, n_sub - 1)), dma((steps, n_sub - 1)),
            dma((steps, n_tm - 1)), dma((steps, n_tm - 1)),
            dma((steps, n_sub - 1)), dma((steps, n_sub - 1)),
        ],
        compiler_params=pltpu.CompilerParams(
            vmem_limit_bytes=48 * 2**20, collective_id=0, has_side_effects=True),
        name="correlate",
    )(spatial_taps, band_edges, source_owner, source_panel, taps, source_pick, raw, spectral_table(), lag_table)


def solution(mesh):
    placed = (
        P(("grp", "chan"), ("tm", "sub")),
        P(),
        P(),
        P(),
        P("grp"),
        P(),
        P(None, ("grp", "chan")),
    )
    return jax.shard_map(
        shards,
        mesh=mesh,
        in_specs=placed,
        out_specs=P(None, ("grp", "chan"), None),
        check_vma=False,
    )
```

```python
import functools
import math

import jax
import jax.numpy as jnp
import numpy as np
from jax import lax
from jax.experimental import pallas as pl
from jax.experimental.pallas import tpu as pltpu
from jax.sharding import PartitionSpec as P

P_SIZE = 32
WIN = 256
LAGS = 128
REACH = 1000
HIGHEST = lax.Precision.HIGHEST


def column_maps():
    column = np.arange(WIN)
    quarter = WIN // 4
    bins = column // (2 * quarter) * quarter + column % quarter
    parts = column // quarter % 2
    return bins, parts


def spectral_table():
    bins, parts = column_maps()
    angle = 2.0 * np.pi * ((bins[None, :] * np.arange(WIN)[:, None]) % WIN) / WIN
    table = np.where(parts == 0, np.cos(angle), -np.sin(angle)) / math.sqrt(WIN)
    return jnp.asarray(table.astype(np.float32)).astype(jnp.bfloat16)


def bins_of(shape, axis):
    column = lax.broadcasted_iota(jnp.int32, shape, axis)
    quarter = WIN // 4
    return lax.div(column, 2 * quarter) * quarter + lax.rem(column, quarter)


def lag_tables(scale):
    bins, parts = column_maps()
    lag = np.arange(LAGS) - LAGS // 2
    angle = 2.0 * np.pi * ((bins[:, None] * lag[None, :]) % WIN) / WIN
    real = np.cos(angle) * scale
    imag = np.where(parts[:, None] == 0, -np.sin(angle), np.sin(angle)) * scale
    return jnp.asarray(np.concatenate([real, imag]).astype(np.float32))


def taper_row(edges_ref):
    bins = bins_of((1, WIN), 1).astype(jnp.float32)
    e0, e1, e2, e3 = [jnp.full((1, WIN), edges_ref[k]).astype(jnp.float32) for k in range(4)]
    rising = 0.5 - 0.5 * jnp.cos(math.pi * (bins - e0) / (e1 - e0))
    falling = 0.5 - 0.5 * jnp.cos(math.pi * (e3 - bins) / (e3 - e2))
    inner = jnp.where(bins < e3, falling, 0.0)
    inner = jnp.where(bins <= e2, 1.0, inner)
    inner = jnp.where(bins < e1, rising, inner)
    return jnp.where(bins <= e0, 0.0, inner)


LANES = 128
SPLIT = 2
LAG = 2
MESH = pl.DeviceIdType.MESH


def kernel(frames, channels, side, steps, n_chan, n_tm, n_sub, sp_hbm, edges_hbm, owner_hbm, panel_hbm,
           taps_hbm, pick_hbm, raw_hbm, table_hbm, lag_hbm, out_ref,
           sp_ref, edges_ref, owner_ref, panel_ref, taps_ref, pick_ref, raw_ref, table_ref, lag_ref, filt, spec, ext, time_in, chan_out, chan_in, corner_out, corner_in, send_sem,
           recv_sem, load_sem, white_ref, own_ref, chosen, pick_wide, plain, swapped, in_low, in_high, to_high,
           to_low, own_lag, sub_in, tm_in, done, sem_high, sem_low, got_low, got_high, sub_send, sub_recv,
           tm_send, tm_recv, fin_send, fin_recv):
    my_tm = lax.axis_index("tm")
    my_sub = lax.axis_index("sub")
    loads = [
        pltpu.make_async_copy(source, target, load_sem.at[k])
        for k, (source, target) in enumerate([
            (raw_hbm, raw_ref), (taps_hbm, taps_ref), (pick_hbm, pick_ref), (sp_hbm, sp_ref),
            (edges_hbm, edges_ref), (owner_hbm, owner_ref), (panel_hbm, panel_ref),
            (table_hbm, table_ref), (lag_hbm, lag_ref),
        ])
    ]
    for load in loads:
        load.start()
    me = lax.axis_index("chan")
    n_time = n_tm * n_sub
    now = lax.axis_index("tm") * n_sub + lax.axis_index("sub")
    samples = frames * WIN
    depth = taps_ref.shape[1]

    def peer(dc, dt):
        at = lax.rem(now + dt + n_time, n_time)
        return {"chan": lax.rem(me + dc + n_chan, n_chan), "tm": lax.div(at, n_sub), "sub": lax.rem(at, n_sub)}

    moves = [(0, 1), (0, -1), (1, 0), (-1, 0), (1, 1), (1, -1), (-1, 1), (-1, -1)]
    barrier = pltpu.get_barrier_semaphore()
    peers = [peer(dc, dt) for dc, dt in moves]
    peers += [{"tm": lax.rem(my_tm + d, n_tm)} for d in range(1, n_tm)]
    peers += [{"sub": lax.rem(my_sub + d, n_sub)} for d in range(1, n_sub)]
    for to in peers:
        pl.semaphore_signal(barrier, inc=1, device_id=to, device_id_type=MESH)

    loads[0].wait()
    ends = (slice(channels - side, channels), slice(0, side))
    sides = (slice(samples - LANES, samples), slice(0, LANES))
    for k in range(2):
        chan_out[k] = raw_ref[ends[k]]
        for h in range(2):
            corner_out[2 * k + h] = raw_ref[ends[k], sides[h]]

    def exists(dc, dt):
        return (me + dc >= 0) & (me + dc < n_chan) & (now + dt >= 0) & (now + dt < n_time)

    def copy(k):
        dc, dt = moves[k]
        if k < 2:
            src, dst = raw_ref.at[:, sides[k]], time_in.at[k]
        elif k < 4:
            src, dst = chan_out.at[k - 2], chan_in.at[k - 2]
        else:
            src, dst = corner_out.at[k - 4], corner_in.at[k - 4]
        return pltpu.make_async_remote_copy(
            src_ref=src, dst_ref=dst, send_sem=send_sem.at[k], recv_sem=recv_sem.at[k],
            device_id=peer(dc, dt), device_id_type=MESH)

    pl.semaphore_wait(barrier, len(peers))
    for k in (2, 3, 0, 1, 4, 5, 6, 7):
        pl.when(exists(*moves[k]))(lambda k=k: copy(k).start())

    ext[:channels, LANES : LANES + samples] = raw_ref[...]
    for load in loads[1:]:
        load.wait()
    rolled = pltpu.roll(jnp.broadcast_to(taps_ref[...], (WIN, depth)), 0, 1, stride=1, stride_axis=0)
    fir_t = rolled.astype(jnp.bfloat16)
    near = (jnp.abs(bins_of((WIN, WIN), 0) - bins_of((WIN, WIN), 1)) <= 4).astype(jnp.float32)
    row_bins = bins_of((1, WIN), 1)
    count = jnp.minimum(row_bins + 4, WIN // 2 - 1) - jnp.maximum(row_bins - 4, 0) + 1
    turned = jnp.transpose(pick_ref[...].astype(jnp.float32))
    for s in range(steps):
        wide = jnp.broadcast_to(turned[:, s : s + 1], (channels, LANES)).astype(jnp.int32)
        pick_wide[s] = wide
        chosen[s] = (
            wide[:, :P_SIZE] == lax.broadcasted_iota(jnp.int32, (channels, P_SIZE), 1)
        ).astype(jnp.bfloat16)

    @pl.when(me == 0)
    def _():
        in_low[...] = jnp.zeros_like(in_low)

    @pl.when(me == n_chan - 1)
    def _():
        in_high[...] = jnp.zeros_like(in_high)

    for k, (dc, dt) in enumerate(moves):
        there = exists(-dc, -dt)
        pl.when(there)(lambda k=k: copy(k).wait_recv())
        buf, slot = (time_in, k) if k < 2 else (chan_in, k - 2) if k < 4 else (corner_in, k - 4)

        @pl.when(jnp.logical_not(there))
        def _():
            buf[slot] = jnp.zeros(buf.shape[1:], buf.dtype)

    def rows(low, high):
        width = low.shape[1]
        spare = jnp.zeros((16 - 2 * side, width), jnp.float32)
        both = [low.astype(jnp.float32), high.astype(jnp.float32), spare]
        return jnp.concatenate(both, axis=0).astype(jnp.bfloat16)

    high_at = LANES + samples
    ext[:channels, :LANES] = time_in[0]
    ext[:channels, high_at:] = time_in[1]
    ext[channels:, LANES:high_at] = rows(chan_in[0], chan_in[1])
    ext[channels:, :LANES] = rows(corner_in[0], corner_in[2])
    ext[channels:, high_at:] = rows(corner_in[1], corner_in[3])
    power = jnp.zeros((channels, WIN), jnp.float32)
    for w in range(frames):
        block = ext[:, w * WIN : w * WIN + depth]
        got = lax.dot_general(block, fir_t, (((1,), (1,)), ((), ())), preferred_element_type=jnp.float32)
        slot = w % 2
        filt[slot, 8 : 8 + channels] = got[:channels]
        filt[slot, 8 - side : 8] = got[channels : channels + side]
        filt[slot, 8 + channels : 8 + channels + side] = got[channels + side : channels + 2 * side]
        shaped = sp_ref[0] * filt[slot, 8 - side : 8 - side + channels]
        for m in range(1, 2 * side + 1):
            shaped += sp_ref[m] * filt[slot, 8 - side + m : 8 - side + m + channels]
        spectra = jnp.dot(shaped.astype(jnp.bfloat16), table_ref[...], preferred_element_type=jnp.float32)
        spec[w] = spectra
        power += spectra * spectra
    level = jnp.dot(power, near, precision=HIGHEST, preferred_element_type=jnp.float32)
    level = level / (count.astype(jnp.float32) * frames)
    factor = taper_row(edges_ref) / jnp.sqrt(level + 1e-06)
    for w in range(frames):
        white_ref[w] = (spec[w] * factor).astype(jnp.bfloat16)
    half = WIN // 2
    part = channels // n_sub
    group = frames // SPLIT
    chunks = steps * SPLIT

    def up(c):
        return pltpu.make_async_remote_copy(
            src_ref=to_high.at[c], dst_ref=in_low.at[c], send_sem=sem_high.at[c], recv_sem=got_low.at[c],
            device_id={"chan": lax.rem(me + 1, n_chan)}, device_id_type=MESH)

    def down(c):
        return pltpu.make_async_remote_copy(
            src_ref=to_low.at[c], dst_ref=in_high.at[c], send_sem=sem_low.at[c], recv_sem=got_high.at[c],
            device_id={"chan": lax.rem(me + n_chan - 1, n_chan)}, device_id_type=MESH)

    def sub_copy(s, d):
        to = lax.rem(my_sub + d, n_sub)
        return pltpu.make_async_remote_copy(
            src_ref=own_lag.at[s, pl.ds(to * part, part)], dst_ref=sub_in.at[s, d - 1],
            send_sem=sub_send.at[s, d - 1], recv_sem=sub_recv.at[s, d - 1],
            device_id={"sub": to}, device_id_type=MESH)

    def tm_copy(s, d):
        return pltpu.make_async_remote_copy(
            src_ref=tm_in.at[s, my_tm], dst_ref=tm_in.at[s, my_tm],
            send_sem=tm_send.at[s, d - 1], recv_sem=tm_recv.at[s, d - 1],
            device_id={"tm": lax.rem(my_tm + d, n_tm)}, device_id_type=MESH)

    def fin_copy(s, d):
        here = pl.ds(my_sub * part, part)
        return pltpu.make_async_remote_copy(
            src_ref=done.at[s, here], dst_ref=done.at[s, here],
            send_sem=fin_send.at[s, d - 1], recv_sem=fin_recv.at[s, d - 1],
            device_id={"sub": lax.rem(my_sub + d, n_sub)}, device_id_type=MESH)

    def own_panel(s):
        panel = jnp.full((P_SIZE, WIN), panel_ref[s], jnp.int32)
        for w in range(frames):
            value = white_ref[w, :P_SIZE]
            for k in range(1, channels // P_SIZE):
                value = jnp.where(panel == k, white_ref[w, k * P_SIZE : (k + 1) * P_SIZE], value)
            own_ref[s, w] = value

    def stage(c, arrived, leaving):
        s = lax.div(c, SPLIT)
        k = lax.rem(c, SPLIT)
        mine = jnp.full((P_SIZE, WIN), owner_ref[s], jnp.int32) == me
        for w in range(group):
            leaving[c, w] = jnp.where(mine, own_ref[s, k * group + w], arrived[c, w])

    def relay(t):
        c = t - LAG * me

        @pl.when((c >= 0) & (c < chunks))
        def _():
            @pl.when(me > 0)
            def _():
                up(c).wait_recv()

            @pl.when(me < n_chan - 1)
            def _():
                stage(c, in_low, to_high)
                up(c).start()

        e = t - LAG * (n_chan - 1 - me)

        @pl.when((e >= 0) & (e < chunks))
        def _():
            @pl.when(me < n_chan - 1)
            def _():
                down(e).wait_recv()

            @pl.when(me > 0)
            def _():
                stage(e, in_high, to_low)
                down(e).start()

    def compute(s):
        rows = channels // 2
        owner = owner_ref[s]
        where = jnp.full((P_SIZE, WIN), owner, jnp.int32)
        start = owner * channels + panel_ref[s] * P_SIZE
        for r in range(2):
            here = slice(r * rows, (r + 1) * rows)
            acc_p = jnp.zeros((rows, WIN), jnp.float32)
            acc_q = jnp.zeros((rows, WIN), jnp.float32)
            for w in range(frames):
                c = s * SPLIT + w // group
                value = jnp.where(where < me, in_low[c, w % group], in_high[c, w % group])
                value = jnp.where(where == me, own_ref[s, w], value)
                partner = jnp.dot(chosen[s, here], value, preferred_element_type=jnp.float32)
                acc_p += plain[w, here] * partner
                acc_q += swapped[w, here] * partner
            lagged = jnp.dot(acc_p, lag_ref[:WIN], precision=HIGHEST, preferred_element_type=jnp.float32)
            lagged += jnp.dot(acc_q, lag_ref[WIN:], precision=HIGHEST, preferred_element_type=jnp.float32)
            receiver = me * channels + r * rows + lax.broadcasted_iota(jnp.int32, (rows, LAGS), 0)
            far = jnp.abs(receiver - (start + pick_wide[s, here])) > REACH
            own_lag[s, here] = jnp.where(far, 0.0, lagged)
        for d in range(1, n_sub):
            sub_copy(s, d).start()

    def sub_sum(s):
        total = own_lag[s, pl.ds(my_sub * part, part)]
        for d in range(1, n_sub):
            sub_copy(s, d).wait_recv()
            total += sub_in[s, d - 1]
        tm_in[s, my_tm] = total
        for d in range(1, n_tm):
            tm_copy(s, d).start()

    def tm_sum(s):
        for d in range(1, n_tm):
            tm_copy(s, d).wait_recv()
        total = tm_in[s, 0]
        for k in range(1, n_tm):
            total += tm_in[s, k]
        done[s, pl.ds(my_sub * part, part)] = total
        for d in range(1, n_sub):
            fin_copy(s, d).start()

    def finish(s):
        for d in range(1, n_sub):
            fin_copy(s, d).wait_recv()
        out_ref[s] = done[s]

    delay = -(-(n_chan - 1) * LAG // SPLIT)

    def turn(u, carry):
        pl.when(u < steps)(functools.partial(own_panel, u))
        for k in range(SPLIT):
            relay(u * SPLIT + k)

        @pl.when(u == 0)
        def _():
            for w in range(frames):
                value = white_ref[w].astype(jnp.float32)
                plain[w] = value
                for h in range(2):
                    swapped[w, :, h * half : (h + 1) * half] = pltpu.roll(
                        value[:, h * half : (h + 1) * half], half // 2, 1)

        for late, work in enumerate((compute, sub_sum, tm_sum, finish)):
            s = u - delay - late
            pl.when((s >= 0) & (s < steps))(functools.partial(work, s))
        return carry

    lax.fori_loop(0, steps + delay + 3, turn, 0)

    def drain_chunk(c, carry):
        @pl.when(me < n_chan - 1)
        def _():
            up(c).wait_send()

        @pl.when(me > 0)
        def _():
            down(c).wait_send()
        return carry

    lax.fori_loop(0, chunks, drain_chunk, 0)
    for k, move in enumerate(moves):
        pl.when(exists(*move))(lambda k=k: copy(k).wait_send())

    def drain_step(s, carry):
        for d in range(1, n_sub):
            sub_copy(s, d).wait_send()
            fin_copy(s, d).wait_send()
        for d in range(1, n_tm):
            tm_copy(s, d).wait_send()
        return carry

    lax.fori_loop(0, steps, drain_step, 0)


VMEM = pl.BlockSpec(memory_space=pltpu.VMEM)


def shards(raw, fir_taps, spatial_taps, band_edges, source_owner, source_panel, source_pick):
    channels, samples = raw.shape
    margin = (fir_taps.shape[0] - 1) // 2
    side = spatial_taps.shape[0] // 2
    frames = samples // WIN
    steps = source_owner.shape[0]
    times = ("tm", "sub")
    count = lax.axis_size(times)
    n_chan = lax.axis_size("chan")
    n_tm, n_sub = lax.axis_size("tm"), lax.axis_size("sub")
    depth = WIN + 2 * LANES
    first = LANES - margin
    taps = jnp.pad(fir_taps.astype(jnp.float32), (first, depth - first - fir_taps.shape[0]))[None, :]
    total = frames * n_tm * n_sub
    lag_table = lag_tables(1.0 / math.sqrt(total * (WIN // 2)))
    chunks = steps * SPLIT
    flow = pltpu.VMEM((chunks, frames // SPLIT, P_SIZE, WIN), jnp.bfloat16)
    part = channels // n_sub
    dma = pltpu.SemaphoreType.DMA
    any_space = pl.BlockSpec(memory_space=pl.ANY)
    bf16, f32 = jnp.bfloat16, jnp.float32
    return pl.pallas_call(
        functools.partial(kernel, frames, channels, side, steps, n_chan, n_tm, n_sub),
        out_shape=jax.ShapeDtypeStruct((steps, channels, LAGS), f32),
        in_specs=[any_space] * 9,
        out_specs=VMEM,
        scratch_shapes=[
            pltpu.SMEM(spatial_taps.shape, f32),
            pltpu.SMEM(band_edges.shape, jnp.int32),
            pltpu.SMEM(source_owner.shape, jnp.int32),
            pltpu.SMEM(source_panel.shape, jnp.int32),
            pltpu.VMEM(taps.shape, f32),
            pltpu.VMEM(source_pick.shape, jnp.int32),
            pltpu.VMEM(raw.shape, bf16),
            pltpu.VMEM((WIN, WIN), bf16),
            pltpu.VMEM((2 * WIN, LAGS), f32),
            pltpu.VMEM((2, channels + 16, WIN), f32),
            pltpu.VMEM((frames, channels, WIN), f32),
            pltpu.VMEM((channels + 16, samples + 2 * LANES), bf16),
            pltpu.VMEM((2, channels, LANES), bf16),
            pltpu.VMEM((2, side, samples), bf16),
            pltpu.VMEM((2, side, samples), bf16),
            pltpu.VMEM((4, side, LANES), bf16),
            pltpu.VMEM((4, side, LANES), bf16),
            dma((8,)), dma((8,)), dma((9,)),
            pltpu.VMEM((frames, channels, WIN), bf16),
            pltpu.VMEM((steps, frames, P_SIZE, WIN), bf16),
            pltpu.VMEM((steps, channels, P_SIZE), bf16),
            pltpu.VMEM((steps, channels, LANES), jnp.int32),
            pltpu.VMEM((frames, channels, WIN), f32),
            pltpu.VMEM((frames, channels, WIN), f32),
            flow, flow, flow, flow,
            pltpu.VMEM((steps, channels, LAGS), f32),
            pltpu.VMEM((steps, n_sub - 1, part, LAGS), f32),
            pltpu.VMEM((steps, n_tm, part, LAGS), f32),
            pltpu.VMEM((steps, channels, LAGS), f32),
            dma((chunks,)), dma((chunks,)), dma((chunks,)), dma((chunks,)),
            dma((steps, n_sub - 1)), dma((steps, n_sub - 1)),
            dma((steps, n_tm - 1)), dma((steps, n_tm - 1)),
            dma((steps, n_sub - 1)), dma((steps, n_sub - 1)),
        ],
        compiler_params=pltpu.CompilerParams(
            vmem_limit_bytes=48 * 2**20, collective_id=0, has_side_effects=True),
        name="correlate",
    )(spatial_taps, band_edges, source_owner, source_panel, taps, source_pick, raw, spectral_table(), lag_table)


def solution(mesh):
    placed = (
        P(("grp", "chan"), ("tm", "sub")),
        P(),
        P(),
        P(),
        P("grp"),
        P(),
        P(None, ("grp", "chan")),
    )
    return jax.shard_map(
        shards,
        mesh=mesh,
        in_specs=placed,
        out_specs=P(None, ("grp", "chan"), None),
        check_vma=False,
    )
```

```python
import functools
import math

import jax
import jax.numpy as jnp
import numpy as np
from jax import lax
from jax.experimental import pallas as pl
from jax.experimental.pallas import tpu as pltpu
from jax.sharding import PartitionSpec as P

P_SIZE = 32
WIN = 256
LAGS = 128
REACH = 1000
HIGHEST = lax.Precision.HIGHEST


def column_maps():
    column = np.arange(WIN)
    quarter = WIN // 4
    bins = column // (2 * quarter) * quarter + column % quarter
    parts = column // quarter % 2
    return bins, parts


def spectral_table():
    bins, parts = column_maps()
    angle = 2.0 * np.pi * ((bins[None, :] * np.arange(WIN)[:, None]) % WIN) / WIN
    table = np.where(parts == 0, np.cos(angle), -np.sin(angle)) / math.sqrt(WIN)
    return jnp.asarray(table.astype(np.float32)).astype(jnp.bfloat16)


def bins_of(shape, axis):
    column = lax.broadcasted_iota(jnp.int32, shape, axis)
    quarter = WIN // 4
    return lax.div(column, 2 * quarter) * quarter + lax.rem(column, quarter)


def lag_tables(scale):
    bins, parts = column_maps()
    lag = np.arange(LAGS) - LAGS // 2
    angle = 2.0 * np.pi * ((bins[:, None] * lag[None, :]) % WIN) / WIN
    real = np.cos(angle) * scale
    imag = np.where(parts[:, None] == 0, -np.sin(angle), np.sin(angle)) * scale
    return jnp.asarray(np.concatenate([real, imag]).astype(np.float32))


def taper_row(edges_ref):
    bins = bins_of((1, WIN), 1).astype(jnp.float32)
    e0, e1, e2, e3 = [jnp.full((1, WIN), edges_ref[k]).astype(jnp.float32) for k in range(4)]
    rising = 0.5 - 0.5 * jnp.cos(math.pi * (bins - e0) / (e1 - e0))
    falling = 0.5 - 0.5 * jnp.cos(math.pi * (e3 - bins) / (e3 - e2))
    inner = jnp.where(bins < e3, falling, 0.0)
    inner = jnp.where(bins <= e2, 1.0, inner)
    inner = jnp.where(bins < e1, rising, inner)
    return jnp.where(bins <= e0, 0.0, inner)


LANES = 128
SPLIT = 2
LAG = 2
MESH = pl.DeviceIdType.MESH


def kernel(frames, channels, side, steps, n_chan, n_tm, n_sub, sp_hbm, edges_hbm, owner_hbm, panel_hbm,
           taps_hbm, pick_hbm, raw_hbm, table_hbm, lag_hbm, out_ref,
           sp_ref, edges_ref, owner_ref, panel_ref, taps_ref, pick_ref, raw_ref, table_ref, lag_ref, filt, spec, ext, time_in, chan_out, chan_in, corner_out, corner_in, send_sem,
           recv_sem, load_sem, white_ref, own_ref, chosen, pick_wide, plain, swapped, in_low, in_high, to_high,
           to_low, own_lag, sub_in, tm_in, done, sem_high, sem_low, got_low, got_high, sub_send, sub_recv,
           tm_send, tm_recv, fin_send, fin_recv):
    my_tm = lax.axis_index("tm")
    my_sub = lax.axis_index("sub")
    loads = [
        pltpu.make_async_copy(source, target, load_sem.at[k])
        for k, (source, target) in enumerate([
            (raw_hbm, raw_ref), (taps_hbm, taps_ref), (pick_hbm, pick_ref), (sp_hbm, sp_ref),
            (edges_hbm, edges_ref), (owner_hbm, owner_ref), (panel_hbm, panel_ref),
            (table_hbm, table_ref), (lag_hbm, lag_ref),
        ])
    ]
    for load in loads:
        load.start()
    me = lax.axis_index("chan")
    n_time = n_tm * n_sub
    now = lax.axis_index("tm") * n_sub + lax.axis_index("sub")
    samples = frames * WIN
    depth = taps_ref.shape[1]

    def peer(dc, dt):
        at = lax.rem(now + dt + n_time, n_time)
        return {"chan": lax.rem(me + dc + n_chan, n_chan), "tm": lax.div(at, n_sub), "sub": lax.rem(at, n_sub)}

    moves = [(0, 1), (0, -1), (1, 0), (-1, 0), (1, 1), (1, -1), (-1, 1), (-1, -1)]
    barrier = pltpu.get_barrier_semaphore()
    peers = [peer(dc, dt) for dc, dt in moves]
    peers += [{"tm": lax.rem(my_tm + d, n_tm)} for d in range(1, n_tm)]
    peers += [{"sub": lax.rem(my_sub + d, n_sub)} for d in range(1, n_sub)]
    for to in peers:
        pl.semaphore_signal(barrier, inc=1, device_id=to, device_id_type=MESH)

    loads[0].wait()
    ends = (slice(channels - side, channels), slice(0, side))
    sides = (slice(samples - LANES, samples), slice(0, LANES))
    for k in range(2):
        chan_out[k] = raw_ref[ends[k]]
        for h in range(2):
            corner_out[2 * k + h] = raw_ref[ends[k], sides[h]]

    def exists(dc, dt):
        return (me + dc >= 0) & (me + dc < n_chan) & (now + dt >= 0) & (now + dt < n_time)

    def copy(k):
        dc, dt = moves[k]
        if k < 2:
            src, dst = raw_ref.at[:, sides[k]], time_in.at[k]
        elif k < 4:
            src, dst = chan_out.at[k - 2], chan_in.at[k - 2]
        else:
            src, dst = corner_out.at[k - 4], corner_in.at[k - 4]
        return pltpu.make_async_remote_copy(
            src_ref=src, dst_ref=dst, send_sem=send_sem.at[k], recv_sem=recv_sem.at[k],
            device_id=peer(dc, dt), device_id_type=MESH)

    pl.semaphore_wait(barrier, len(peers))
    for k in (2, 3, 0, 1, 4, 5, 6, 7):
        pl.when(exists(*moves[k]))(lambda k=k: copy(k).start())

    ext[:channels, LANES : LANES + samples] = raw_ref[...]
    for load in loads[1:]:
        load.wait()
    rolled = pltpu.roll(jnp.broadcast_to(taps_ref[...], (WIN, depth)), 0, 1, stride=1, stride_axis=0)
    fir_t = rolled.astype(jnp.bfloat16)
    near = (jnp.abs(bins_of((WIN, WIN), 0) - bins_of((WIN, WIN), 1)) <= 4).astype(jnp.float32)
    row_bins = bins_of((1, WIN), 1)
    count = jnp.minimum(row_bins + 4, WIN // 2 - 1) - jnp.maximum(row_bins - 4, 0) + 1
    turned = jnp.transpose(pick_ref[...].astype(jnp.float32))
    for s in range(steps):
        wide = jnp.broadcast_to(turned[:, s : s + 1], (channels, LANES)).astype(jnp.int32)
        pick_wide[s] = wide
        chosen[s] = (
            wide[:, :P_SIZE] == lax.broadcasted_iota(jnp.int32, (channels, P_SIZE), 1)
        ).astype(jnp.bfloat16)

    @pl.when(me == 0)
    def _():
        in_low[...] = jnp.zeros_like(in_low)

    @pl.when(me == n_chan - 1)
    def _():
        in_high[...] = jnp.zeros_like(in_high)

    for k, (dc, dt) in enumerate(moves):
        there = exists(-dc, -dt)
        pl.when(there)(lambda k=k: copy(k).wait_recv())
        buf, slot = (time_in, k) if k < 2 else (chan_in, k - 2) if k < 4 else (corner_in, k - 4)

        @pl.when(jnp.logical_not(there))
        def _():
            buf[slot] = jnp.zeros(buf.shape[1:], buf.dtype)

    def rows(low, high):
        width = low.shape[1]
        spare = jnp.zeros((16 - 2 * side, width), jnp.float32)
        both = [low.astype(jnp.float32), high.astype(jnp.float32), spare]
        return jnp.concatenate(both, axis=0).astype(jnp.bfloat16)

    high_at = LANES + samples
    ext[:channels, :LANES] = time_in[0]
    ext[:channels, high_at:] = time_in[1]
    ext[channels:, LANES:high_at] = rows(chan_in[0], chan_in[1])
    ext[channels:, :LANES] = rows(corner_in[0], corner_in[2])
    ext[channels:, high_at:] = rows(corner_in[1], corner_in[3])
    power = jnp.zeros((channels, WIN), jnp.float32)
    for w in range(frames):
        block = ext[:, w * WIN : w * WIN + depth]
        got = lax.dot_general(block, fir_t, (((1,), (1,)), ((), ())), preferred_element_type=jnp.float32)
        slot = w % 2
        filt[slot, 8 : 8 + channels] = got[:channels]
        filt[slot, 8 - side : 8] = got[channels : channels + side]
        filt[slot, 8 + channels : 8 + channels + side] = got[channels + side : channels + 2 * side]
        shaped = sp_ref[0] * filt[slot, 8 - side : 8 - side + channels]
        for m in range(1, 2 * side + 1):
            shaped += sp_ref[m] * filt[slot, 8 - side + m : 8 - side + m + channels]
        spectra = jnp.dot(shaped.astype(jnp.bfloat16), table_ref[...], preferred_element_type=jnp.float32)
        spec[w] = spectra
        power += spectra * spectra
    level = jnp.dot(power, near, precision=HIGHEST, preferred_element_type=jnp.float32)
    level = level / (count.astype(jnp.float32) * frames)
    factor = taper_row(edges_ref) / jnp.sqrt(level + 1e-06)
    for w in range(frames):
        white_ref[w] = (spec[w] * factor).astype(jnp.bfloat16)
    half = WIN // 2
    part = channels // n_sub
    group = frames // SPLIT
    chunks = steps * SPLIT

    def up(c):
        return pltpu.make_async_remote_copy(
            src_ref=to_high.at[c], dst_ref=in_low.at[c], send_sem=sem_high.at[c], recv_sem=got_low.at[c],
            device_id={"chan": lax.rem(me + 1, n_chan)}, device_id_type=MESH)

    def down(c):
        return pltpu.make_async_remote_copy(
            src_ref=to_low.at[c], dst_ref=in_high.at[c], send_sem=sem_low.at[c], recv_sem=got_high.at[c],
            device_id={"chan": lax.rem(me + n_chan - 1, n_chan)}, device_id_type=MESH)

    def sub_copy(s, d):
        to = lax.rem(my_sub + d, n_sub)
        return pltpu.make_async_remote_copy(
            src_ref=own_lag.at[s, pl.ds(to * part, part)], dst_ref=sub_in.at[s, d - 1],
            send_sem=sub_send.at[s, d - 1], recv_sem=sub_recv.at[s, d - 1],
            device_id={"sub": to}, device_id_type=MESH)

    def tm_copy(s, d):
        return pltpu.make_async_remote_copy(
            src_ref=tm_in.at[s, my_tm], dst_ref=tm_in.at[s, my_tm],
            send_sem=tm_send.at[s, d - 1], recv_sem=tm_recv.at[s, d - 1],
            device_id={"tm": lax.rem(my_tm + d, n_tm)}, device_id_type=MESH)

    def fin_copy(s, d):
        here = pl.ds(my_sub * part, part)
        return pltpu.make_async_remote_copy(
            src_ref=done.at[s, here], dst_ref=done.at[s, here],
            send_sem=fin_send.at[s, d - 1], recv_sem=fin_recv.at[s, d - 1],
            device_id={"sub": lax.rem(my_sub + d, n_sub)}, device_id_type=MESH)

    def own_panel(s):
        panel = jnp.full((P_SIZE, WIN), panel_ref[s], jnp.int32)
        for w in range(frames):
            value = white_ref[w, :P_SIZE]
            for k in range(1, channels // P_SIZE):
                value = jnp.where(panel == k, white_ref[w, k * P_SIZE : (k + 1) * P_SIZE], value)
            own_ref[s, w] = value

    def stage(c, arrived, leaving):
        s = lax.div(c, SPLIT)
        k = lax.rem(c, SPLIT)
        mine = jnp.full((P_SIZE, WIN), owner_ref[s], jnp.int32) == me
        for w in range(group):
            leaving[c, w] = jnp.where(mine, own_ref[s, k * group + w], arrived[c, w])

    def relay(t):
        c = t - LAG * me

        @pl.when((c >= 0) & (c < chunks))
        def _():
            @pl.when(me > 0)
            def _():
                up(c).wait_recv()

            @pl.when(me < n_chan - 1)
            def _():
                stage(c, in_low, to_high)
                up(c).start()

        e = t - LAG * (n_chan - 1 - me)

        @pl.when((e >= 0) & (e < chunks))
        def _():
            @pl.when(me < n_chan - 1)
            def _():
                down(e).wait_recv()

            @pl.when(me > 0)
            def _():
                stage(e, in_high, to_low)
                down(e).start()

    def compute(s):
        rows = channels // 2
        owner = owner_ref[s]
        where = jnp.full((P_SIZE, WIN), owner, jnp.int32)
        start = owner * channels + panel_ref[s] * P_SIZE
        for r in range(2):
            here = slice(r * rows, (r + 1) * rows)
            acc_p = jnp.zeros((rows, WIN), jnp.float32)
            acc_q = jnp.zeros((rows, WIN), jnp.float32)
            for w in range(frames):
                c = s * SPLIT + w // group
                value = jnp.where(where < me, in_low[c, w % group], in_high[c, w % group])
                value = jnp.where(where == me, own_ref[s, w], value)
                partner = jnp.dot(chosen[s, here], value, preferred_element_type=jnp.float32)
                acc_p += plain[w, here] * partner
                acc_q += swapped[w, here] * partner
            lagged = jnp.dot(acc_p, lag_ref[:WIN], precision=HIGHEST, preferred_element_type=jnp.float32)
            lagged += jnp.dot(acc_q, lag_ref[WIN:], precision=HIGHEST, preferred_element_type=jnp.float32)
            receiver = me * channels + r * rows + lax.broadcasted_iota(jnp.int32, (rows, LAGS), 0)
            far = jnp.abs(receiver - (start + pick_wide[s, here])) > REACH
            own_lag[s, here] = jnp.where(far, 0.0, lagged)
        for d in range(1, n_sub):
            sub_copy(s, d).start()

    def sub_sum(s):
        total = own_lag[s, pl.ds(my_sub * part, part)]
        for d in range(1, n_sub):
            sub_copy(s, d).wait_recv()
            total += sub_in[s, d - 1]
        tm_in[s, my_tm] = total
        for d in range(1, n_tm):
            tm_copy(s, d).start()

    def tm_sum(s):
        for d in range(1, n_tm):
            tm_copy(s, d).wait_recv()
        total = tm_in[s, 0]
        for k in range(1, n_tm):
            total += tm_in[s, k]
        done[s, pl.ds(my_sub * part, part)] = total
        for d in range(1, n_sub):
            fin_copy(s, d).start()

    def finish(s):
        for d in range(1, n_sub):
            fin_copy(s, d).wait_recv()
        out_ref[s] = done[s]

    delay = -(-(n_chan - 1) * LAG // SPLIT)

    def turn(u, carry):
        pl.when(u < steps)(functools.partial(own_panel, u))
        for k in range(SPLIT):
            relay(u * SPLIT + k)

        @pl.when(u == 0)
        def _():
            for w in range(frames):
                value = white_ref[w].astype(jnp.float32)
                plain[w] = value
                for h in range(2):
                    swapped[w, :, h * half : (h + 1) * half] = pltpu.roll(
                        value[:, h * half : (h + 1) * half], half // 2, 1)

        for late, work in enumerate((compute, sub_sum, tm_sum, finish)):
            s = u - delay - late
            pl.when((s >= 0) & (s < steps))(functools.partial(work, s))
        return carry

    lax.fori_loop(0, steps + delay + 3, turn, 0)

    def drain_chunk(c, carry):
        @pl.when(me < n_chan - 1)
        def _():
            up(c).wait_send()

        @pl.when(me > 0)
        def _():
            down(c).wait_send()
        return carry

    lax.fori_loop(0, chunks, drain_chunk, 0)
    for k, move in enumerate(moves):
        pl.when(exists(*move))(lambda k=k: copy(k).wait_send())

    def drain_step(s, carry):
        for d in range(1, n_sub):
            sub_copy(s, d).wait_send()
            fin_copy(s, d).wait_send()
        for d in range(1, n_tm):
            tm_copy(s, d).wait_send()
        return carry

    lax.fori_loop(0, steps, drain_step, 0)


VMEM = pl.BlockSpec(memory_space=pltpu.VMEM)


def shards(raw, fir_taps, spatial_taps, band_edges, source_owner, source_panel, source_pick):
    channels, samples = raw.shape
    margin = (fir_taps.shape[0] - 1) // 2
    side = spatial_taps.shape[0] // 2
    frames = samples // WIN
    steps = source_owner.shape[0]
    times = ("tm", "sub")
    count = lax.axis_size(times)
    n_chan = lax.axis_size("chan")
    n_tm, n_sub = lax.axis_size("tm"), lax.axis_size("sub")
    depth = WIN + 2 * LANES
    first = LANES - margin
    taps = jnp.pad(fir_taps.astype(jnp.float32), (first, depth - first - fir_taps.shape[0]))[None, :]
    total = frames * n_tm * n_sub
    lag_table = lag_tables(1.0 / math.sqrt(total * (WIN // 2)))
    chunks = steps * SPLIT
    flow = pltpu.VMEM((chunks, frames // SPLIT, P_SIZE, WIN), jnp.bfloat16)
    part = channels // n_sub
    dma = pltpu.SemaphoreType.DMA
    any_space = pl.BlockSpec(memory_space=pltpu.HBM)
    bf16, f32 = jnp.bfloat16, jnp.float32
    return pl.pallas_call(
        functools.partial(kernel, frames, channels, side, steps, n_chan, n_tm, n_sub),
        out_shape=jax.ShapeDtypeStruct((steps, channels, LAGS), f32),
        in_specs=[any_space] * 9,
        out_specs=VMEM,
        scratch_shapes=[
            pltpu.SMEM(spatial_taps.shape, f32),
            pltpu.SMEM(band_edges.shape, jnp.int32),
            pltpu.SMEM(source_owner.shape, jnp.int32),
            pltpu.SMEM(source_panel.shape, jnp.int32),
            pltpu.VMEM(taps.shape, f32),
            pltpu.VMEM(source_pick.shape, jnp.int32),
            pltpu.VMEM(raw.shape, bf16),
            pltpu.VMEM((WIN, WIN), bf16),
            pltpu.VMEM((2 * WIN, LAGS), f32),
            pltpu.VMEM((2, channels + 16, WIN), f32),
            pltpu.VMEM((frames, channels, WIN), f32),
            pltpu.VMEM((channels + 16, samples + 2 * LANES), bf16),
            pltpu.VMEM((2, channels, LANES), bf16),
            pltpu.VMEM((2, side, samples), bf16),
            pltpu.VMEM((2, side, samples), bf16),
            pltpu.VMEM((4, side, LANES), bf16),
            pltpu.VMEM((4, side, LANES), bf16),
            dma((8,)), dma((8,)), dma((9,)),
            pltpu.VMEM((frames, channels, WIN), bf16),
            pltpu.VMEM((steps, frames, P_SIZE, WIN), bf16),
            pltpu.VMEM((steps, channels, P_SIZE), bf16),
            pltpu.VMEM((steps, channels, LANES), jnp.int32),
            pltpu.VMEM((frames, channels, WIN), f32),
            pltpu.VMEM((frames, channels, WIN), f32),
            flow, flow, flow, flow,
            pltpu.VMEM((steps, channels, LAGS), f32),
            pltpu.VMEM((steps, n_sub - 1, part, LAGS), f32),
            pltpu.VMEM((steps, n_tm, part, LAGS), f32),
            pltpu.VMEM((steps, channels, LAGS), f32),
            dma((chunks,)), dma((chunks,)), dma((chunks,)), dma((chunks,)),
            dma((steps, n_sub - 1)), dma((steps, n_sub - 1)),
            dma((steps, n_tm - 1)), dma((steps, n_tm - 1)),
            dma((steps, n_sub - 1)), dma((steps, n_sub - 1)),
        ],
        compiler_params=pltpu.CompilerParams(
            vmem_limit_bytes=64 * 2**20, collective_id=0, has_side_effects=True),
        name="correlate",
    )(spatial_taps, band_edges, source_owner, source_panel, taps, source_pick, raw, spectral_table(), lag_table)


def solution(mesh):
    placed = (
        P(("grp", "chan"), ("tm", "sub")),
        P(),
        P(),
        P(),
        P("grp"),
        P(),
        P(None, ("grp", "chan")),
    )
    return jax.shard_map(
        shards,
        mesh=mesh,
        in_specs=placed,
        out_specs=P(None, ("grp", "chan"), None),
        check_vma=False,
    )
```
